128 devices in a mesh: dp: 64 (over z, y, x), expert: 2 (over core).
Axes of the slice: x: 4, y: 4, z: 4, core: 2. Of those that a mesh axis runs over, the one named last changes fastest.
Arguments:
- hidden: bfloat16 [2, 65536, 1024], P('expert', 'dp'), may hold values from -6 to 6
- cotangent: bfloat16 [2, 65536, 3584], P('expert', 'dp'), may hold values from -6 to 6
- counts: int32 [2, 64], P('expert', 'dp'), may hold values from 1 to 1024, as said below
- placement: int32 [2, 4], replicated, may hold values from 0 to 1, as said below
- weight: bfloat16 [2, 1024, 3584], P('expert', 'dp'), may hold values from -4 to 4
- moment: float32 [2, 1024, 3584], P('expert', 'dp'), may hold values from -2 to 2
- second: float32 [2, 1024, 3584], P('expert', 'dp'), may hold values from 0.005 to 1
- serving: bfloat16 [2, 4, 1024, 3584], P('expert', None, 'dp'), may hold values from -4 to 4
Outputs:
- d_hidden: bfloat16 [2, 65536, 1024], P('expert', 'dp')
- new_weight: bfloat16 [2, 1024, 3584], P('expert', 'dp')
- new_moment: float32 [2, 1024, 3584], P('expert', 'dp')
- new_second: float32 [2, 1024, 3584], P('expert', 'dp')
- served: bfloat16 [2, 4, 1024, 3584], P('expert', None, 'dp')
The draws below stay inside these ranges and needn't reach their ends.
Inputs may be any that keep to these rules, and one draw needn't show every extreme that they name: `counts`: every count is reached by some expert and data shard in every draw at its upper end, 1024. `placement`: some two groups hold different experts as their first replica.
All inputs are finite; a program needn't handle non-finite values.
Results may differ from the reference program's by a relative error of at most 0.0012.
Values may be sent and summed in bfloat16 or wider, within the bound.
A program may use at most 128 MiB of HBM per device.

```python
import math
import jax
import jax.numpy as jnp
from jax import lax

D = 3584
FF = 1024
TOK = 1024
REPL = 4
EXPERTS = 2
N_DP = 64


def draw_counts(key, part):
    key_level, key_base, key_row, key_col = jax.random.split(jax.random.fold_in(key, 17), 4)
    level = jax.random.randint(key_level, (EXPERTS, 1), 1, 5)
    base = jax.random.randint(key_base, (EXPERTS, N_DP), TOK // 8, TOK // 4 + 1)
    loads = jnp.minimum(base * level, TOK)
    row_pick = jax.random.randint(key_row, (), 0, EXPERTS)
    col_pick = jax.random.randint(key_col, (), 0, N_DP)
    loads = loads.at[row_pick, col_pick].set(TOK)
    return loads.astype(jnp.int32)


def draw_placement(key, part):
    key_base, key_pick, key_shift = jax.random.split(jax.random.fold_in(key, 29), 3)
    groups = jax.random.randint(key_base, (EXPERTS, REPL), 0, EXPERTS)
    chosen = jax.random.randint(key_pick, (), 0, EXPERTS)
    neighbour = groups[(chosen + 1) % EXPERTS, 0]
    offset = jax.random.randint(key_shift, (), 1, EXPERTS)
    groups = groups.at[chosen, 0].set((neighbour + offset) % EXPERTS)
    return groups.astype(jnp.int32)


def levels(own_key, extent, cuts, low, top_value):
    level, own = 1.0, jax.random.fold_in(own_key, 6)
    for axis_at, shards_of in cuts:
        heights = jnp.exp(jax.random.uniform(jax.random.fold_in(own, axis_at), (shards_of,), jnp.float32, low / len(cuts), top_value / len(cuts)))
        level = level * jnp.repeat(heights, extent[axis_at] // shards_of).reshape([-1 if axis == axis_at else 1 for axis in range(len(extent))])
    return level


def bell_draw(rng, extent, deviation, most, shards=(), held_as=jnp.bfloat16):
    values = deviation * jax.random.normal(rng, extent, jnp.float32)
    if shards:
        values = values * levels(rng, extent, shards, -0.22, 0.18)
    return jnp.clip(values, -most, most).astype(held_as)


def setup_inputs(seed: int = 0) -> dict:
    seeds = jax.random.split(jax.random.key(seed), 9)
    hidden = bell_draw(seeds[0], (EXPERTS, N_DP * TOK, FF), 1.0, 6.0, ((0, 2), (1, 64)))
    cotangent = bell_draw(seeds[1], (EXPERTS, N_DP * TOK, D), 1.0, 6.0, ((0, 2), (1, 64)))
    counts = draw_counts(jax.random.fold_in(seeds[8], 71), 0)
    placement = draw_placement(jax.random.fold_in(seeds[8], 71), 0)
    weight = bell_draw(seeds[4], (EXPERTS, FF, D), 1.0, 4.0, ((0, 2), (1, 64)))
    moment = bell_draw(seeds[5], (EXPERTS, FF, D), 0.3, 2.0, ((0, 2), (1, 64)), jnp.float32)
    second = jnp.clip(jnp.exp(math.log(1.0) - 5.2983174 * jax.random.uniform(seeds[6], (EXPERTS, FF, D), jnp.float32) ** levels(seeds[6], (EXPERTS, FF, D), ((0, 2), (1, 64)), -0.2, 0.2)), 0.005, 1.0)
    serving = bell_draw(seeds[7], (EXPERTS, REPL, FF, D), 1.0, 4.0, ((0, 2), (2, 64)))
    return dict(hidden=hidden, cotangent=cotangent, counts=counts, placement=placement, weight=weight, moment=moment, second=second, serving=serving)


beta_one = 0.9
beta_two = 0.95
bias_one = 1.0 - 0.9 ** 20
bias_two = 1.0 - 0.95 ** 20
learn_rate = 0.05
decay_rate = 0.1
epsilon = 1e-08

def reference(hidden, cotangent, counts, placement, weight, moment, second, serving):
    scale = D ** (-0.5)
    slots = jnp.arange(N_DP * TOK, dtype=jnp.int32)
    position = slots % TOK
    shard = slots // TOK

    def one_expert(operands):
        acts, grads_out, limit, matrix, first, squares = operands
        live = position < limit[shard]
        masked = jnp.where(live[:, None], grads_out, jnp.zeros_like(grads_out))
        d_hid = (scale * jnp.dot(masked, matrix.T, preferred_element_type=jnp.float32)).astype(jnp.bfloat16)
        grad = scale * jnp.dot(acts.T, masked, preferred_element_type=jnp.float32)
        first_new = beta_one * first + (1.0 - beta_one) * grad
        squares_new = beta_two * squares + (1.0 - beta_two) * grad * grad
        step = first_new / bias_one / (jnp.sqrt(squares_new / bias_two) + epsilon)
        current = matrix.astype(jnp.float32)
        updated = current - learn_rate * (step + decay_rate * current)
        delta = (updated - current).astype(jnp.bfloat16)
        return (d_hid, updated.astype(jnp.bfloat16), first_new, squares_new, delta)
    d_hidden, new_weight, new_moment, new_second, delta = lax.map(one_expert, (hidden, cotangent, counts, weight, moment, second))
    picked = jnp.take(delta, placement.astype(jnp.int32), axis=0)
    served = (serving.astype(jnp.float32) + picked.astype(jnp.float32)).astype(jnp.bfloat16)
    return (d_hidden, new_weight, new_moment, new_second, served)
```

```python
import functools

import jax
import jax.numpy as jnp
from jax import lax
from jax.experimental import pallas as pl
from jax.experimental.pallas import tpu as pltpu
from jax.sharding import Mesh
from jax.sharding import PartitionSpec as P

DP = ("dp_0", "dp_1", "dp_2")
MESH = pl.DeviceIdType.MESH
RING = 4

beta_one = 0.9
beta_two = 0.95
bias_one = 1.0 - 0.9**20
bias_two = 1.0 - 0.95**20
learn_rate = 0.05
decay_rate = 0.1
epsilon = 1e-08

TILE = 256
TOP = 32767.0
LANES = 3
GATHER = ((2, 1, 0), (0, 2, 1), (1, 0, 2))
SCATTER = ((0, 1, 2), (1, 2, 0), (2, 0, 1))


def lane_columns(width):
    tiles = width // TILE
    low = tiles // LANES
    counts = [low + (1 if lane < tiles - low * LANES else 0) for lane in range(LANES)]
    starts = [sum(counts[:lane]) * TILE for lane in range(LANES)]
    return tuple((start, count * TILE) for start, count in zip(starts, counts))


def fused(
    scale, lanes,
    counts, placement, hid_in, cot_in, w_in, mom_in, sec_in, srv_in,
    dh_out, nw_out, nm_out, ns_out, so_out,
    weights, hid, hid_t, cot, grads, mom, sec, srv, nw, nm, ns, so, delta,
    sent1, got1, sent2, got2, sent3, got3,
    sent1_top, got1_top, sent2_top, got2_top, sent3_top, got3_top,
    ga_send, ga_recv, gb_send, gb_recv, gc_send, gc_recv,
    r1_send, r1_recv, r1t_send, r1t_recv,
    r2_send, r2_recv, r2t_send, r2t_recv,
    r3_send, r3_recv, r3t_send, r3t_recv,
    d_send, d_recv, in_sem, dh_sem, out_sem,
):
    me = tuple(lax.axis_index(name) for name in DP)
    core = lax.axis_index("expert")
    tokens = hid.shape[0]
    owned = weights.shape[3]

    def on_ring(axis, offset):
        return lax.rem(me[axis] + (offset + RING) % RING, RING)

    def remote(src, dst, send, recv, axis, offset):
        return pltpu.make_async_remote_copy(
            src_ref=src, dst_ref=dst, send_sem=send, recv_sem=recv,
            device_id={DP[axis]: on_ring(axis, offset)}, device_id_type=MESH,
        )

    def block(ref, at, columns=None):
        index = tuple(at.get(axis, slice(None)) for axis in range(3))
        if columns is None:
            return ref.at[index]
        return ref.at[index + (slice(None), pl.ds(*columns))]

    load_w = pltpu.make_async_copy(w_in, weights.at[me[0], me[1], me[2]], in_sem.at[0])
    load_hid = pltpu.make_async_copy(hid_in, hid, in_sem.at[1])
    load_cot = pltpu.make_async_copy(cot_in, cot, in_sem.at[2])
    load_mom = pltpu.make_async_copy(mom_in, mom, in_sem.at[3])
    load_sec = pltpu.make_async_copy(sec_in, sec, in_sem.at[4])
    load_srv = pltpu.make_async_copy(srv_in, srv, in_sem.at[5])
    for load in (load_w, load_hid, load_cot, load_mom, load_sec, load_srv):
        load.start()

    barrier = pltpu.get_barrier_semaphore()
    for axis in range(3):
        for offset in range(1, RING):
            pl.semaphore_signal(
                barrier, inc=1, device_id={DP[axis]: on_ring(axis, offset)}, device_id_type=MESH
            )
    pl.semaphore_signal(barrier, inc=1, device_id={"expert": 1 - core}, device_id_type=MESH)
    pl.semaphore_wait(barrier, 3 * (RING - 1) + 1)

    started = []

    def start(copy):
        copy.start()
        started.append(copy)
        return copy

    def gather_small(stage, send, recv):
        copies = [[] for _ in range(LANES)]
        for offset in (1, 3, 2):
            for lane in range(LANES):
                order = GATHER[lane]
                axis = order[stage]
                at = {other: me[other] for other in order[stage:]}
                part = block(weights, at, lanes[lane])
                copies[lane].append(
                    start(remote(part, part, send.at[lane, offset - 1], recv.at[lane, offset - 1], axis, offset))
                )
        return copies

    def arrive(copies):
        for lane in copies:
            for copy in lane:
                copy.wait_recv()

    def half(order_axis, which):
        return {order_axis: pl.ds(2 * which, 2)}

    def gather_large_first():
        copies = []
        for lane in range(LANES):
            mid, axis = GATHER[lane][1], GATHER[lane][2]
            row = []
            for slot, (offset, which) in enumerate(((1, 0), (3, 1), (1, 1), (3, 0))):
                part = block(weights, {axis: me[axis], **half(mid, which)}, lanes[lane])
                row.append(start(remote(part, part, gc_send.at[lane, slot], gc_recv.at[lane, slot], axis, offset)))
            copies.append(row)
        return copies

    def gather_large_second(first):
        copies = []
        for lane in range(LANES):
            mid, axis = GATHER[lane][1], GATHER[lane][2]
            row = []
            for slot, (offset, which) in enumerate(((1, 0), (3, 1))):
                first[lane][slot].wait_recv()
                part = block(weights, {axis: on_ring(axis, -offset), **half(mid, which)}, lanes[lane])
                row.append(start(remote(part, part, gc_send.at[lane, 4 + slot], gc_recv.at[lane, 4 + slot], axis, offset)))
            copies.append(row)
        return copies

    load_w.wait()
    first = gather_small(0, ga_send, ga_recv)

    load_hid.wait()
    limit = counts[0, 0]

    def turn(step):
        rows = pl.ds(pl.multiple_of(step * TILE, TILE), TILE)
        slots = lax.broadcasted_iota(jnp.int32, (TILE, 1), 0) + step * TILE
        piece = jnp.where(slots < limit, hid[rows, :].astype(jnp.float32), 0.0)
        hid_t[:, rows] = piece.T.astype(hid_t.dtype)

    def tiles(count, body):
        def step(at, carry):
            body(at)
            return carry
        lax.fori_loop(0, count, step, 0)

    tiles(tokens // TILE // 2, turn)
    arrive(first)
    second = gather_small(1, gb_send, gb_recv)
    tiles(tokens // TILE - tokens // TILE // 2, lambda at: turn(at + tokens // TILE // 2))

    def product(lane, low, high):
        begin = lanes[lane][0]

        def body(at):
            columns = pl.ds(pl.multiple_of(begin + (low + at) * TILE, TILE), TILE)
            value = jnp.dot(hid_t[...], cot[:, columns], preferred_element_type=jnp.float32)
            grads[:, :, :, :, columns] = value.reshape(RING, RING, RING, owned, TILE)
        tiles(high - low, body)

    def encode(read, count, write, top_ref):
        def largest(at, top):
            return jnp.maximum(top, jnp.abs(read(at)))
        shape = read(0).shape
        top = lax.fori_loop(0, count, largest, jnp.zeros(shape, jnp.float32))
        top = jnp.maximum(jnp.max(top, keepdims=True), 1e-30)
        factor = TOP / top

        def code(at):
            write(at, jnp.round(read(at) * factor).astype(jnp.int32).astype(jnp.int16))
        tiles(count, code)
        top_ref[...] = jnp.broadcast_to(top * (1.0 / TOP), top_ref.shape)

    def three(order, first_at, second_at, third_at):
        at = {order[0]: first_at, order[1]: second_at, order[2]: third_at}
        return at[0], at[1], at[2]

    MESSAGES = ((2, 0, 1), (1, 1, 1), (1, 0, 1), (2, 1, 3), (3, 0, 3), (3, 1, 3))

    def scatter_large(lane, message, forwarded):
        order = SCATTER[lane]
        begin, width = lanes[lane]
        owner, which, way = MESSAGES[message]
        row = on_ring(order[0], owner)

        def read(at):
            z, y, x = three(order, row, 2 * which + at // RING, at % RING)
            value = grads[z, y, x, :, pl.ds(begin, width)]
            if forwarded is not None:
                value += decoded(got1.at[lane, forwarded], got1_top.at[lane, forwarded], lane, at)
            return value

        def write(at, value):
            sent1[lane, message, at, :, pl.ds(0, width)] = value

        if forwarded is not None:
            def add(at):
                z, y, x = three(order, row, 2 * which + at // RING, at % RING)
                grads[z, y, x, :, pl.ds(begin, width)] = read(at)
            tiles(2 * RING, add)
            encode(lambda at: grads[three(order, row, 2 * which + at // RING, at % RING) + (slice(None), pl.ds(begin, width))],
                   2 * RING, write, sent1_top.at[lane, message])
        else:
            encode(read, 2 * RING, write, sent1_top.at[lane, message])
        columns = pl.ds(0, width)
        return (
            start(remote(sent1_top.at[lane, message], got1_top.at[lane, message],
                         r1t_send.at[lane, message], r1t_recv.at[lane, message], order[0], way)),
            start(remote(sent1.at[lane, message, :, :, columns], got1.at[lane, message, :, :, columns],
                         r1_send.at[lane, message], r1_recv.at[lane, message], order[0], way)),
        )

    def decoded(codes, top_ref, lane, at):
        width = lanes[lane][1]
        return codes[at, :, pl.ds(0, width)].astype(jnp.float32) * top_ref[0:1, 0:1]

    def landed(pair):
        pair[0].wait_recv()
        pair[1].wait_recv()

    tile_count = [width // TILE for _, width in lanes]
    large = [dict() for _ in range(LANES)]

    load_cot.wait()
    product(0, 0, 2)
    arrive(second)
    third = gather_large_first()
    product(0, 2, tile_count[0])
    for message in (0, 3):
        large[0][message] = scatter_large(0, message, None)
    product(1, 0, tile_count[1])
    for message in (0, 3):
        large[1][message] = scatter_large(1, message, None)
    product(2, 0, tile_count[2])
    for message in (0, 3):
        large[2][message] = scatter_large(2, message, None)
    fourth = gather_large_second(third)
    for lane in range(LANES):
        for message in (1, 4):
            large[lane][message] = scatter_large(lane, message, None)

    limit_mask = lax.broadcasted_iota(jnp.int32, (tokens, 1), 0) < limit
    quarter = RING * RING * owned

    def d_hidden(at):
        rows = weights[at].reshape(quarter, weights.shape[4])
        value = lax.dot_general(
            cot[...], rows, (((1,), (1,)), ((), ())), preferred_element_type=jnp.float32
        )
        value = jnp.where(limit_mask, scale * value, 0.0)
        hid[:, pl.ds(pl.multiple_of(at * quarter, quarter), quarter)] = value.astype(hid.dtype)

    for lane in range(LANES):
        for slot in (2, 3):
            third[lane][slot].wait_recv()
    arrive(fourth)
    tiles(2, d_hidden)

    for lane in range(LANES):
        landed(large[lane][0])
        large[lane][2] = scatter_large(lane, 2, 0)
        landed(large[lane][3])
        large[lane][5] = scatter_large(lane, 5, 3)

    tiles(2, lambda at: d_hidden(at + 2))
    store_dh = pltpu.make_async_copy(hid, dh_out, dh_sem.at[0])
    store_dh.start()

    medium = [[] for _ in range(LANES)]
    for lane in range(LANES):
        order = SCATTER[lane]
        begin, width = lanes[lane]
        for message in (1, 4, 2, 5):
            landed(large[lane][message])

        for which, (near, far) in enumerate(((4, 2), (1, 5))):
            def add(at, which=which, near=near, far=far):
                z, y, x = three(order, me[order[0]], 2 * which + at // RING, at % RING)
                grads[z, y, x, :, pl.ds(begin, width)] = (
                    grads[z, y, x, :, pl.ds(begin, width)]
                    + decoded(got1.at[lane, near], got1_top.at[lane, near], lane, at)
                    + decoded(got1.at[lane, far], got1_top.at[lane, far], lane, at)
                )
            tiles(2 * RING, add)
        for offset in (2, 1, 3):
            slot = offset - 1

            def read(at):
                z, y, x = three(order, me[order[0]], on_ring(order[1], offset), at)
                return grads[z, y, x, :, pl.ds(begin, width)]

            def write(at, value):
                sent2[lane, slot, at, :, pl.ds(0, width)] = value
            encode(read, RING, write, sent2_top.at[lane, slot])
            columns = pl.ds(0, width)
            medium[lane].append((
                start(remote(sent2_top.at[lane, slot], got2_top.at[lane, slot],
                             r2t_send.at[lane, slot], r2t_recv.at[lane, slot], order[1], offset)),
                start(remote(sent2.at[lane, slot, :, :, columns], got2.at[lane, slot, :, :, columns],
                             r2_send.at[lane, slot], r2_recv.at[lane, slot], order[1], offset)),
            ))

    small = [[] for _ in range(LANES)]
    for lane in range(LANES):
        order = SCATTER[lane]
        begin, width = lanes[lane]
        for pair in medium[lane]:
            landed(pair)

        def add(at):
            z, y, x = three(order, me[order[0]], me[order[1]], at)
            value = grads[z, y, x, :, pl.ds(begin, width)]
            for slot in range(RING - 1):
                value += decoded(got2.at[lane, slot], got2_top.at[lane, slot], lane, at)
            grads[z, y, x, :, pl.ds(begin, width)] = value
        tiles(RING, add)
        for offset in (2, 1, 3):
            slot = offset - 1

            def read(at):
                z, y, x = three(order, me[order[0]], me[order[1]], on_ring(order[2], offset))
                return grads[z, y, x, :, pl.ds(begin, width)]

            def write(at, value):
                sent3[lane, slot, at, :, pl.ds(0, width)] = value
            encode(read, 1, write, sent3_top.at[lane, slot])
            columns = pl.ds(0, width)
            small[lane].append((
                start(remote(sent3_top.at[lane, slot], got3_top.at[lane, slot],
                             r3t_send.at[lane, slot], r3t_recv.at[lane, slot], order[2], offset)),
                start(remote(sent3.at[lane, slot, :, :, columns], got3.at[lane, slot, :, :, columns],
                             r3_send.at[lane, slot], r3_recv.at[lane, slot], order[2], offset)),
            ))

    for load in (load_mom, load_sec, load_srv):
        load.wait()
    shared = []
    stores = []
    for lane in range(LANES):
        begin, width = lanes[lane]
        columns = pl.ds(begin, width)
        for pair in small[lane]:
            landed(pair)
        total = grads[me[0], me[1], me[2], :, columns]
        for slot in range(RING - 1):
            total += decoded(got3.at[lane, slot], got3_top.at[lane, slot], lane, 0)
        grad = scale * total
        first_new = beta_one * mom[:, columns] + (1.0 - beta_one) * grad
        squares_new = beta_two * sec[:, columns] + (1.0 - beta_two) * grad * grad
        step = first_new / bias_one / (jnp.sqrt(squares_new / bias_two) + epsilon)
        current = weights[me[0], me[1], me[2], :, columns].astype(jnp.float32)
        updated = current - learn_rate * (step + decay_rate * current)
        delta[core, :, columns] = (updated - current).astype(delta.dtype)
        part = delta.at[core, :, columns]
        shared.append(start(pltpu.make_async_remote_copy(
            src_ref=part, dst_ref=part, send_sem=d_send.at[lane], recv_sem=d_recv.at[lane],
            device_id={"expert": 1 - core}, device_id_type=MESH,
        )))
        nw[:, columns] = updated.astype(nw.dtype)
        nm[:, columns] = first_new
        ns[:, columns] = squares_new
        for slot, (src, dst) in enumerate(((nw, nw_out), (nm, nm_out), (ns, ns_out))):
            store = pltpu.make_async_copy(src.at[:, columns], dst.at[:, columns], out_sem.at[lane, slot])
            store.start()
            stores.append(store)
    for lane in range(LANES):
        begin, width = lanes[lane]
        columns = pl.ds(begin, width)
        shared[lane].wait_recv()
        choices = [delta[expert, :, columns].astype(jnp.float32) for expert in range(2)]
        for replica in range(srv.shape[0]):
            pick = jnp.full((owned, width), placement[core, replica], jnp.int32) == 0
            incoming = jnp.where(pick, choices[0], choices[1])
            so[replica, :, columns] = (srv[replica, :, columns].astype(jnp.float32) + incoming).astype(so.dtype)
        store = pltpu.make_async_copy(so.at[:, :, columns], so_out.at[:, :, columns], out_sem.at[lane, 3])
        store.start()
        stores.append(store)
    for copy in started:
        copy.wait_send()
    for store in stores:
        store.wait()
    store_dh.wait()


def on_device(hidden, cotangent, counts, placement, weight, moment, second, serving):
    tokens, rows = hidden.shape[1:]
    width = cotangent.shape[2]
    owned = weight.shape[1]
    copies = serving.shape[1]
    lanes = lane_columns(width)
    widest = max(count for _, count in lanes)
    scale = width ** (-0.5)
    anywhere = pl.BlockSpec(memory_space=pl.ANY)
    scalars = pl.BlockSpec(memory_space=pltpu.SMEM)
    f32, bf16, i16 = jnp.float32, jnp.bfloat16, jnp.int16
    dma = pltpu.SemaphoreType.DMA
    outs = pl.pallas_call(
        functools.partial(fused, scale, lanes),
        out_shape=(
            jax.ShapeDtypeStruct((tokens, rows), bf16),
            jax.ShapeDtypeStruct((owned, width), bf16),
            jax.ShapeDtypeStruct((owned, width), f32),
            jax.ShapeDtypeStruct((owned, width), f32),
            jax.ShapeDtypeStruct((copies, owned, width), bf16),
        ),
        in_specs=[scalars, scalars] + [anywhere] * 6,
        out_specs=[anywhere] * 5,
        scratch_shapes=[
            pltpu.VMEM((RING, RING, RING, owned, width), bf16),
            pltpu.VMEM((tokens, rows), bf16),
            pltpu.VMEM((rows, tokens), bf16),
            pltpu.VMEM((tokens, width), bf16),
            pltpu.VMEM((RING, RING, RING, owned, width), f32),
            pltpu.VMEM((owned, width), f32),
            pltpu.VMEM((owned, width), f32),
            pltpu.VMEM((copies, owned, width), bf16),
            pltpu.VMEM((owned, width), bf16),
            pltpu.VMEM((owned, width), f32),
            pltpu.VMEM((owned, width), f32),
            pltpu.VMEM((copies, owned, width), bf16),
            pltpu.VMEM((2, owned, width), bf16),
            pltpu.VMEM((LANES, 6, 2 * RING, owned, widest), i16),
            pltpu.VMEM((LANES, 6, 2 * RING, owned, widest), i16),
            pltpu.VMEM((LANES, 3, RING, owned, widest), i16),
            pltpu.VMEM((LANES, 3, RING, owned, widest), i16),
            pltpu.VMEM((LANES, 3, 1, owned, widest), i16),
            pltpu.VMEM((LANES, 3, 1, owned, widest), i16),
            pltpu.VMEM((LANES, 6, 8, 128), f32),
            pltpu.VMEM((LANES, 6, 8, 128), f32),
            pltpu.VMEM((LANES, 3, 8, 128), f32),
            pltpu.VMEM((LANES, 3, 8, 128), f32),
            pltpu.VMEM((LANES, 3, 8, 128), f32),
            pltpu.VMEM((LANES, 3, 8, 128), f32),
        ]
        + [dma((LANES, 3))] * 4
        + [dma((LANES, 6))] * 2
        + [dma((LANES, 6))] * 4
        + [dma((LANES, 3))] * 8
        + [dma((LANES,))] * 2
        + [dma((6,)), dma((1,)), dma((LANES, 4))],
        compiler_params=pltpu.CompilerParams(
            collective_id=0, has_side_effects=True, vmem_limit_bytes=62 * 2**20
        ),
        cost_estimate=pl.CostEstimate(flops=4 * tokens * rows * width, bytes_accessed=2**25, transcendentals=0),
    )(counts, placement, hidden[0], cotangent[0], weight[0], moment[0], second[0], serving[0])
    return tuple(out[None] for out in outs)


def solution(mesh):
    torus = Mesh(
        mesh.devices.reshape(RING, RING, RING, mesh.shape["expert"]), ("dp_0", "dp_1", "dp_2", "expert")
    )
    return jax.shard_map(
        on_device,
        mesh=torus,
        in_specs=(
            P("expert", DP, None),
            P("expert", DP, None),
            P("expert", DP),
            P(),
            P("expert", DP, None),
            P("expert", DP, None),
            P("expert", DP, None),
            P("expert", None, DP, None),
        ),
        out_specs=(
            P("expert", DP, None),
            P("expert", DP, None),
            P("expert", DP, None),
            P("expert", DP, None),
            P("expert", None, DP, None),
        ),
        check_vma=False,
    )
```

```python
import functools

import jax
import jax.numpy as jnp
from jax import lax
from jax.experimental import pallas as pl
from jax.experimental.pallas import tpu as pltpu
from jax.sharding import Mesh
from jax.sharding import PartitionSpec as P

DP = ("dp_0", "dp_1", "dp_2")
MESH = pl.DeviceIdType.MESH
RING = 4

beta_one = 0.9
beta_two = 0.95
bias_one = 1.0 - 0.9**20
bias_two = 1.0 - 0.95**20
learn_rate = 0.05
decay_rate = 0.1
epsilon = 1e-08

TILE = 256
TOP = 32767.0
LANES = 3
GATHER = ((2, 1, 0), (0, 2, 1), (1, 0, 2))
SCATTER = ((0, 1, 2), (1, 2, 0), (2, 0, 1))


def lane_columns(width, wider):
    tiles = width // 128
    low = tiles // LANES
    counts = [low] * LANES
    for at in range(tiles - low * LANES):
        counts[(wider + at) % LANES] += 1
    starts = [sum(counts[:lane]) * 128 for lane in range(LANES)]
    return tuple((start, count * 128) for start, count in zip(starts, counts))


def fused(
    scale, gather_lanes, lanes,
    counts, placement, hid_in, cot_in, w_in, mom_in, sec_in, srv_in,
    dh, nw, nm, ns, so,
    weights, hid, hid_t, cot, grads, mom, sec, srv, delta,
    sent1, got1, sent2, got2, sent3, got3,
    sent1_top, got1_top, sent2_top, got2_top, sent3_top, got3_top,
    ga_send, ga_recv, gb_send, gb_recv, gc_send, gc_recv,
    r1_send, r1_recv, r1t_send, r1t_recv,
    r2_send, r2_recv, r2t_send, r2t_recv,
    r3_send, r3_recv, r3t_send, r3t_recv,
    d_send, d_recv, in_sem,
):
    me = tuple(lax.axis_index(name) for name in DP)
    core = lax.axis_index("expert")
    tokens = hid.shape[0]
    owned = weights.shape[3]

    def on_ring(axis, offset):
        return lax.rem(me[axis] + (offset + RING) % RING, RING)

    def remote(src, dst, send, recv, axis, offset):
        return pltpu.make_async_remote_copy(
            src_ref=src, dst_ref=dst, send_sem=send, recv_sem=recv,
            device_id={DP[axis]: on_ring(axis, offset)}, device_id_type=MESH,
        )

    def block(at, columns):
        index = tuple(at.get(axis, slice(None)) for axis in range(3))
        return weights.at[index + (slice(None), pl.ds(*columns))]

    load_w = pltpu.make_async_copy(w_in, weights.at[me[0], me[1], me[2]], in_sem.at[0])
    load_hid = pltpu.make_async_copy(hid_in, hid, in_sem.at[1])
    load_cot = pltpu.make_async_copy(cot_in, cot, in_sem.at[2])
    load_mom = pltpu.make_async_copy(mom_in, mom, in_sem.at[3])
    load_sec = pltpu.make_async_copy(sec_in, sec, in_sem.at[4])
    load_srv = pltpu.make_async_copy(srv_in, srv, in_sem.at[5])
    for load in (load_w, load_hid, load_cot, load_mom, load_sec, load_srv):
        load.start()

    barrier = pltpu.get_barrier_semaphore()
    for axis in range(3):
        for offset in range(1, RING):
            pl.semaphore_signal(
                barrier, inc=1, device_id={DP[axis]: on_ring(axis, offset)}, device_id_type=MESH
            )
    pl.semaphore_signal(barrier, inc=1, device_id={"expert": 1 - core}, device_id_type=MESH)
    pl.semaphore_wait(barrier, 3 * (RING - 1) + 1)

    def tiles(count, body):
        def step(at, carry):
            body(at)
            return carry
        lax.fori_loop(0, count, step, 0)

    def part_of(step):
        return jnp.where(step == 0, 2, jnp.where(step == 1, 1, jnp.where(step == 2, 3, 0)))

    def way_of(k):
        return 1 + 2 * lax.rem(k, 2)

    def gather_small(lane, stage, offset, send, recv):
        order = GATHER[lane]
        part = block({axis: me[axis] for axis in order[stage:]}, gather_lanes[lane])
        return remote(part, part, send.at[lane, offset - 1], recv.at[lane, offset - 1], order[stage], offset)

    def gather_large(lane, k, slot):
        _, mid, axis = GATHER[lane]
        way = way_of(k)
        holder = on_ring(axis, -way) if slot == 2 else me[axis]
        part = block({mid: on_ring(mid, k), axis: holder}, gather_lanes[lane])
        offset = RING - way if slot == 1 else way
        return remote(part, part, gc_send.at[lane, k, slot], gc_recv.at[lane, k, slot], axis, offset)

    limit = counts[0, 0]

    def turn(step):
        rows = pl.ds(pl.multiple_of(step * TILE, TILE), TILE)
        slots = lax.broadcasted_iota(jnp.int32, (TILE, 1), 0) + step * TILE
        piece = jnp.where(slots < limit, hid[rows, :].astype(jnp.float32), 0.0)
        hid_t[:, rows] = piece.T.astype(hid_t.dtype)

    def product(at):
        columns = pl.ds(pl.multiple_of(at * TILE, TILE), TILE)
        value = jnp.dot(hid_t[...], cot[:, columns], preferred_element_type=jnp.float32)
        grads[:, :, :, :, columns] = value.reshape(RING, RING, RING, owned, TILE)

    def place(order, first_at, second_at, third_at):
        at = {order[0]: first_at, order[1]: second_at, order[2]: third_at}
        return at[0], at[1], at[2]

    def spread(tile, width):
        rows = jnp.concatenate([tile] * (owned // 8), axis=0)
        return jnp.concatenate([rows] * (width // 128), axis=1)

    def decoded(codes, top_ref, lane, at):
        width = lanes[lane][1]
        return codes[at, :, pl.ds(0, width)].astype(jnp.float32) * spread(top_ref[...], width)

    def encode(lane, where, count, parts, codes, top_ref):
        begin, width = lanes[lane]
        columns = pl.ds(begin, width)

        def largest(at, top):
            index = where(at) + (slice(None), columns)
            value = grads[index]
            for part in parts:
                value += decoded(part[0], part[1], lane, at)
            if parts:
                grads[index] = value
            return jnp.maximum(top, jnp.abs(value))
        top = lax.fori_loop(0, count, largest, jnp.zeros((owned, width), jnp.float32))
        top = largest_piece(top)
        factor = TOP / top
        top_ref[...] = top * (1.0 / TOP)

        def code(at):
            value = grads[where(at) + (slice(None), columns)]
            codes[at, :, pl.ds(0, width)] = jnp.round(value * spread(factor, width)).astype(jnp.int32).astype(jnp.int16)
        tiles(count, code)

    def code_copies(lane, slot, buffers, sems, axis, offset):
        sent, sent_top, got, got_top = buffers
        columns = pl.ds(0, lanes[lane][1])
        return (
            remote(sent_top.at[slot], got_top.at[slot], sems[2].at[slot], sems[3].at[slot], axis, offset),
            remote(sent.at[slot + (slice(None), slice(None), columns)],
                   got.at[slot + (slice(None), slice(None), columns)],
                   sems[0].at[slot], sems[1].at[slot], axis, offset),
        )

    def begin_all(pair):
        for copy in pair:
            copy.start()

    def landed(pair):
        for copy in pair:
            copy.wait_recv()

    def gone(pair):
        for copy in pair:
            copy.wait_send()

    buffers1 = (sent1, sent1_top, got1, got1_top)
    buffers2 = (sent2, sent2_top, got2, got2_top)
    buffers3 = (sent3, sent3_top, got3, got3_top)
    sems1 = (r1_send, r1_recv, r1t_send, r1t_recv)
    sems2 = (r2_send, r2_recv, r2t_send, r2t_recv)
    sems3 = (r3_send, r3_recv, r3t_send, r3t_recv)

    def large(lane, k, message):
        way = way_of(k)
        return code_copies(lane, (lane, k, message), buffers1, sems1, SCATTER[lane][0],
                           RING - way if message == 1 else way)

    def medium(lane, k):
        return code_copies(lane, (lane, k - 1), buffers2, sems2, SCATTER[lane][1], k)

    def small(lane, k):
        return code_copies(lane, (lane, k - 1), buffers3, sems3, SCATTER[lane][2], k)

    def scatter_large(lane, k, message):
        order = SCATTER[lane]
        way = way_of(k)
        row = on_ring(order[0], (2, RING - way, way)[message])
        middle = on_ring(order[1], k)
        parts = []
        if message == 2:
            landed(large(lane, k, 0))
            parts = [(got1.at[lane, k, 0], got1_top.at[lane, k, 0])]
        encode(lane, lambda at: place(order, row, middle, at), RING, parts,
               sent1.at[lane, k, message], sent1_top.at[lane, k, message])
        begin_all(large(lane, k, message))

    def near_parts(lane, k):
        for message in (1, 2):
            landed(large(lane, k, message))
        return [(got1.at[lane, k, message], got1_top.at[lane, k, message]) for message in (1, 2)]

    def scatter_middle(lane, k):
        order = SCATTER[lane]
        middle = on_ring(order[1], k)
        encode(lane, lambda at: place(order, me[order[0]], middle, at), RING, near_parts(lane, k),
               sent2.at[lane, k - 1], sent2_top.at[lane, k - 1])
        begin_all(medium(lane, k))

    def own_parts(lane):
        parts = near_parts(lane, 0)
        for k in range(1, RING):
            landed(medium(lane, k))
            parts.append((got2.at[lane, k - 1], got2_top.at[lane, k - 1]))
        return parts

    def own_value(lane, parts, at):
        order = SCATTER[lane]
        value = grads[place(order, me[order[0]], me[order[1]], at) + (slice(None), pl.ds(*lanes[lane]))]
        for part in parts:
            value += decoded(part[0], part[1], lane, at)
        return value

    def largest_piece(top):
        pieces = [top[row : row + 8, column : column + 128]
                  for row in range(0, top.shape[0], 8) for column in range(0, top.shape[1], 128)]
        while len(pieces) > 1:
            pieces = [jnp.maximum(*pieces[at : at + 2]) if at + 1 < len(pieces) else pieces[at]
                      for at in range(0, len(pieces), 2)]
        return jnp.maximum(pieces[0], 1e-30)

    def scatter_small(lane, k, parts):
        width = lanes[lane][1]
        value = own_value(lane, parts, on_ring(SCATTER[lane][2], k))
        top = largest_piece(jnp.abs(value))
        sent3_top[lane, k - 1] = top * (1.0 / TOP)
        sent3[lane, k - 1, 0, :, pl.ds(0, width)] = (
            jnp.round(value * spread(TOP / top, width)).astype(jnp.int32).astype(jnp.int16)
        )
        begin_all(small(lane, k))

    limit_mask = lax.broadcasted_iota(jnp.int32, (tokens, 1), 0) < limit
    quarter = RING * RING * owned

    def d_hidden(at):
        rows = weights[at].reshape(quarter, weights.shape[4])
        value = lax.dot_general(
            cot[...], rows, (((1,), (1,)), ((), ())), preferred_element_type=jnp.float32
        )
        value = jnp.where(limit_mask, scale * value, 0.0)
        dh[:, pl.ds(pl.multiple_of(at * quarter, quarter), quarter)] = value.astype(dh.dtype)

    every = range(LANES)

    load_w.wait()
    for offset in (1, 3, 2):
        for lane in every:
            gather_small(lane, 0, offset, ga_send, ga_recv).start()
    load_hid.wait()
    tiles(tokens // TILE, turn)
    for offset in (1, 3, 2):
        for lane in every:
            gather_small(lane, 0, offset, ga_send, ga_recv).wait_recv()
    for offset in (1, 3, 2):
        for lane in every:
            gather_small(lane, 1, offset, gb_send, gb_recv).start()
    for slot in range(2):
        for lane in every:
            gather_large(lane, 0, slot).start()
    load_cot.wait()
    tiles(cot.shape[1] // TILE, product)
    for offset in (3, 1, 2):
        for lane in every:
            gather_small(lane, 1, offset, gb_send, gb_recv).wait_recv()
        for slot in range(2):
            for lane in every:
                gather_large(lane, RING - offset, slot).start()

    def near_and_far(step):
        k = part_of(step)
        for lane in every:
            scatter_large(lane, k, 0)
            scatter_large(lane, k, 1)
    tiles(RING, near_and_far)

    def onward(step):
        k = part_of(step)
        for lane in every:
            gather_large(lane, lax.rem(k + 2, RING), 0).wait_recv()
            gather_large(lane, lax.rem(k + 2, RING), 2).start()
        for lane in every:
            scatter_large(lane, k, 2)
    tiles(RING, onward)

    def gathered(k):
        for lane in every:
            gather_large(lane, k, 1).wait_recv()
            gather_large(lane, k, 2).wait_recv()
    tiles(RING, gathered)

    def second_half(step):
        d_hidden(step)

        @pl.when(step < RING - 1)
        def _():
            k = part_of(step)
            for lane in every:
                scatter_middle(lane, k)
    tiles(RING, second_half)
    for lane in every:
        parts = own_parts(lane)
        tiles(RING - 1, lambda step, lane=lane, parts=parts: scatter_small(lane, part_of(step), parts))

    for load in (load_mom, load_sec, load_srv):
        load.wait()
    shared = []
    for lane in range(LANES):
        begin, width = lanes[lane]
        columns = pl.ds(begin, width)
        parts = [(got1.at[lane, 0, message], got1_top.at[lane, 0, message]) for message in (1, 2)]
        parts += [(got2.at[lane, slot], got2_top.at[lane, slot]) for slot in range(RING - 1)]
        total = own_value(lane, parts, me[SCATTER[lane][2]])
        for slot in range(RING - 1):
            landed(small(lane, slot + 1))
            total += decoded(got3.at[lane, slot], got3_top.at[lane, slot], lane, 0)
        grad = scale * total
        first_new = beta_one * mom[:, columns] + (1.0 - beta_one) * grad
        squares_new = beta_two * sec[:, columns] + (1.0 - beta_two) * grad * grad
        step = first_new / bias_one / (jnp.sqrt(squares_new / bias_two) + epsilon)
        current = weights[me[0], me[1], me[2], :, columns].astype(jnp.float32)
        updated = current - learn_rate * (step + decay_rate * current)
        delta[core, :, columns] = (updated - current).astype(delta.dtype)
        part = delta.at[core, :, columns]
        shared.append(pltpu.make_async_remote_copy(
            src_ref=part, dst_ref=part, send_sem=d_send.at[lane], recv_sem=d_recv.at[lane],
            device_id={"expert": 1 - core}, device_id_type=MESH,
        ))
        shared[lane].start()
        nw[:, columns] = updated.astype(nw.dtype)
        nm[:, columns] = first_new
        ns[:, columns] = squares_new
    for lane in range(LANES):
        begin, width = lanes[lane]
        columns = pl.ds(begin, width)
        shared[lane].wait_recv()
        choices = [delta[expert, :, columns].astype(jnp.float32) for expert in range(2)]
        for replica in range(srv.shape[0]):
            pick = jnp.full((owned, width), placement[core, replica], jnp.int32) == 0
            incoming = jnp.where(pick, choices[0], choices[1])
            so[replica, :, columns] = (srv[replica, :, columns].astype(jnp.float32) + incoming).astype(so.dtype)

    def sent_all(k):
        for lane in every:
            for slot in range(3):
                gather_large(lane, k, slot).wait_send()
                gone(large(lane, k, slot))

            @pl.when(k > 0)
            def _():
                gather_small(lane, 0, k, ga_send, ga_recv).wait_send()
                gather_small(lane, 1, k, gb_send, gb_recv).wait_send()
                gone(medium(lane, k))
                gone(small(lane, k))
    tiles(RING, sent_all)
    for copy in shared:
        copy.wait_send()


def on_device(hidden, cotangent, counts, placement, weight, moment, second, serving):
    tokens, rows = hidden.shape[1:]
    width = cotangent.shape[2]
    owned = weight.shape[1]
    copies = serving.shape[1]
    gather_lanes = lane_columns(width, 0)
    lanes = lane_columns(width, 1)
    widest = max(count for _, count in lanes)
    scale = width ** (-0.5)
    anywhere = pl.BlockSpec(memory_space=pl.ANY)
    scalars = pl.BlockSpec(memory_space=pltpu.SMEM)
    f32, bf16, i16 = jnp.float32, jnp.bfloat16, jnp.int16
    dma = pltpu.SemaphoreType.DMA
    outs = pl.pallas_call(
        functools.partial(fused, scale, gather_lanes, lanes),
        out_shape=(
            pltpu.VMEM((tokens, rows), bf16),
            pltpu.VMEM((owned, width), bf16),
            pltpu.VMEM((owned, width), f32),
            pltpu.VMEM((owned, width), f32),
            pltpu.VMEM((copies, owned, width), bf16),
        ),
        in_specs=[scalars, scalars] + [anywhere] * 6,
        out_specs=[pl.BlockSpec(memory_space=pltpu.VMEM)] * 5,
        scratch_shapes=[
            pltpu.VMEM((RING, RING, RING, owned, width), bf16),
            pltpu.VMEM((tokens, rows), bf16),
            pltpu.VMEM((rows, tokens), bf16),
            pltpu.VMEM((tokens, width), bf16),
            pltpu.VMEM((RING, RING, RING, owned, width), f32),
            pltpu.VMEM((owned, width), f32),
            pltpu.VMEM((owned, width), f32),
            pltpu.VMEM((copies, owned, width), bf16),
            pltpu.VMEM((2, owned, width), bf16),
            pltpu.VMEM((LANES, RING, 3, RING, owned, widest), i16),
            pltpu.VMEM((LANES, RING, 3, RING, owned, widest), i16),
            pltpu.VMEM((LANES, 3, RING, owned, widest), i16),
            pltpu.VMEM((LANES, 3, RING, owned, widest), i16),
            pltpu.VMEM((LANES, 3, 1, owned, widest), i16),
            pltpu.VMEM((LANES, 3, 1, owned, widest), i16),
            pltpu.VMEM((LANES, RING, 3, 8, 128), f32),
            pltpu.VMEM((LANES, RING, 3, 8, 128), f32),
            pltpu.VMEM((LANES, 3, 8, 128), f32),
            pltpu.VMEM((LANES, 3, 8, 128), f32),
            pltpu.VMEM((LANES, 3, 8, 128), f32),
            pltpu.VMEM((LANES, 3, 8, 128), f32),
        ]
        + [dma((LANES, 3))] * 4
        + [dma((LANES, RING, 3))] * 6
        + [dma((LANES, 3))] * 8
        + [dma((LANES,))] * 2
        + [dma((6,))],
        compiler_params=pltpu.CompilerParams(
            collective_id=0, has_side_effects=True, vmem_limit_bytes=56 * 2**20
        ),
        cost_estimate=pl.CostEstimate(flops=4 * tokens * rows * width, bytes_accessed=2**25, transcendentals=0),
    )(counts, placement, hidden[0], cotangent[0], weight[0], moment[0], second[0], serving[0])
    return tuple(out[None] for out in outs)


def solution(mesh):
    torus = Mesh(
        mesh.devices.reshape(RING, RING, RING, mesh.shape["expert"]), ("dp_0", "dp_1", "dp_2", "expert")
    )
    return jax.shard_map(
        on_device,
        mesh=torus,
        in_specs=(
            P("expert", DP, None),
            P("expert", DP, None),
            P("expert", DP),
            P(),
            P("expert", DP, None),
            P("expert", DP, None),
            P("expert", DP, None),
            P("expert", None, DP, None),
        ),
        out_specs=(
            P("expert", DP, None),
            P("expert", DP, None),
            P("expert", DP, None),
            P("expert", DP, None),
            P("expert", None, DP, None),
        ),
        check_vma=False,
    )
```

```python
import functools

import jax
import jax.numpy as jnp
from jax import lax
from jax.experimental import pallas as pl
from jax.experimental.pallas import tpu as pltpu
from jax.sharding import Mesh
from jax.sharding import PartitionSpec as P

DP = ("dp_0", "dp_1", "dp_2")
MESH = pl.DeviceIdType.MESH
RING = 4

beta_one = 0.9
beta_two = 0.95
bias_one = 1.0 - 0.9**20
bias_two = 1.0 - 0.95**20
learn_rate = 0.05
decay_rate = 0.1
epsilon = 1e-08

TILE = 256
TOP = 32767.0
LANES = 3
GATHER = ((2, 1, 0), (0, 2, 1), (1, 0, 2))
SCATTER = ((0, 1, 2), (1, 2, 0), (2, 0, 1))


def lane_columns(width, wider):
    tiles = width // 128
    low = tiles // LANES
    counts = [low] * LANES
    for at in range(tiles - low * LANES):
        counts[(wider + at) % LANES] += 1
    starts = [sum(counts[:lane]) * 128 for lane in range(LANES)]
    return tuple((start, count * 128) for start, count in zip(starts, counts))


def fused(
    scale, gather_lanes, lanes,
    counts, placement, hid_in, cot_in, w_in, mom_in, sec_in, srv_in,
    dh, nw, nm, ns, so,
    weights, hid, hid_t, cot, grads, dh_t, mom, sec, srv, delta,
    sent1, got1, sent2, got2, sent3, got3,
    sent1_top, got1_top, sent2_top, got2_top, sent3_top, got3_top,
    ga_send, ga_recv, gb_send, gb_recv, gc_send, gc_recv,
    r1_send, r1_recv, r1t_send, r1t_recv,
    r2_send, r2_recv, r2t_send, r2t_recv,
    r3_send, r3_recv, r3t_send, r3t_recv,
    d_send, d_recv, in_sem,
):
    me = tuple(lax.axis_index(name) for name in DP)
    core = lax.axis_index("expert")
    tokens = hid.shape[0]
    owned = weights.shape[3]

    def on_ring(axis, offset):
        return lax.rem(me[axis] + (offset + RING) % RING, RING)

    def remote(src, dst, send, recv, axis, offset):
        return pltpu.make_async_remote_copy(
            src_ref=src, dst_ref=dst, send_sem=send, recv_sem=recv,
            device_id={DP[axis]: on_ring(axis, offset)}, device_id_type=MESH,
        )

    def block(at, columns):
        index = tuple(at.get(axis, slice(None)) for axis in range(3))
        return weights.at[index + (slice(None), pl.ds(*columns))]

    barrier = pltpu.get_barrier_semaphore()
    for axis in range(3):
        for offset in range(1, RING):
            pl.semaphore_signal(
                barrier, inc=1, device_id={DP[axis]: on_ring(axis, offset)}, device_id_type=MESH
            )
    pl.semaphore_signal(barrier, inc=1, device_id={"expert": 1 - core}, device_id_type=MESH)

    load_w = pltpu.make_async_copy(w_in, weights.at[me[0], me[1], me[2]], in_sem.at[0])
    load_hid = pltpu.make_async_copy(hid_in, hid, in_sem.at[1])
    load_cot = pltpu.make_async_copy(cot_in, cot, in_sem.at[2])
    load_mom = pltpu.make_async_copy(mom_in, mom, in_sem.at[3])
    load_sec = pltpu.make_async_copy(sec_in, sec, in_sem.at[4])
    load_srv = pltpu.make_async_copy(srv_in, srv, in_sem.at[5])
    for load in (load_w, load_hid, load_cot, load_mom, load_sec, load_srv):
        load.start()

    pl.semaphore_wait(barrier, 3 * (RING - 1) + 1)

    def tiles(count, body):
        def step(at, carry):
            body(at)
            return carry
        lax.fori_loop(0, count, step, 0)

    def part_of(step):
        return jnp.where(step == 0, 2, jnp.where(step == 1, 1, jnp.where(step == 2, 3, 0)))

    def way_of(k):
        return 1 + 2 * lax.rem(k, 2)

    def gather_small(lane, stage, offset, send, recv):
        order = GATHER[lane]
        part = block({axis: me[axis] for axis in order[stage:]}, gather_lanes[lane])
        return remote(part, part, send.at[lane, offset - 1], recv.at[lane, offset - 1], order[stage], offset)

    def gather_large(lane, k, slot):
        _, mid, axis = GATHER[lane]
        way = way_of(k)
        holder = on_ring(axis, -way) if slot == 2 else me[axis]
        part = block({mid: on_ring(mid, k), axis: holder}, gather_lanes[lane])
        offset = RING - way if slot == 1 else way
        return remote(part, part, gc_send.at[lane, k, slot], gc_recv.at[lane, k, slot], axis, offset)

    limit = counts[0, 0]

    def turn(step):
        rows = pl.ds(pl.multiple_of(step * TILE, TILE), TILE)
        slots = lax.broadcasted_iota(jnp.int32, (TILE, 1), 0) + step * TILE
        piece = jnp.where(slots < limit, hid[rows, :].astype(jnp.float32), 0.0)
        hid_t[:, rows] = piece.T.astype(hid_t.dtype)

    def product(at):
        columns = pl.ds(pl.multiple_of(at * TILE, TILE), TILE)
        value = jnp.dot(hid_t[...], cot[:, columns], preferred_element_type=jnp.float32)
        grads[:, :, :, :, columns] = value.reshape(RING, RING, RING, owned, TILE)

    def place(order, first_at, second_at, third_at):
        at = {order[0]: first_at, order[1]: second_at, order[2]: third_at}
        return at[0], at[1], at[2]

    def spread(tile, width):
        rows = jnp.concatenate([tile] * (owned // 8), axis=0)
        return jnp.concatenate([rows] * (width // 128), axis=1)

    def decoded(codes, top_ref, lane, at):
        width = lanes[lane][1]
        return codes[at, :, pl.ds(0, width)].astype(jnp.float32) * spread(top_ref[...], width)

    def encode(lane, where, count, parts, codes, top_ref):
        begin, width = lanes[lane]
        columns = pl.ds(begin, width)

        def largest(at, top):
            index = where(at) + (slice(None), columns)
            value = grads[index]
            for part in parts:
                value += decoded(part[0], part[1], lane, at)
            if parts:
                grads[index] = value
            return jnp.maximum(top, jnp.abs(value))
        top = lax.fori_loop(0, count, largest, jnp.zeros((owned, width), jnp.float32))
        top = largest_piece(top)
        factor = TOP / top
        top_ref[...] = top * (1.0 / TOP)

        def code(at):
            value = grads[where(at) + (slice(None), columns)]
            codes[at, :, pl.ds(0, width)] = jnp.round(value * spread(factor, width)).astype(jnp.int32).astype(jnp.int16)
        tiles(count, code)

    def code_copies(lane, slot, buffers, sems, axis, offset):
        sent, sent_top, got, got_top = buffers
        columns = pl.ds(0, lanes[lane][1])
        return (
            remote(sent_top.at[slot], got_top.at[slot], sems[2].at[slot], sems[3].at[slot], axis, offset),
            remote(sent.at[slot + (slice(None), slice(None), columns)],
                   got.at[slot + (slice(None), slice(None), columns)],
                   sems[0].at[slot], sems[1].at[slot], axis, offset),
        )

    def begin_all(pair):
        for copy in pair:
            copy.start()

    def landed(pair):
        for copy in pair:
            copy.wait_recv()

    def gone(pair):
        for copy in pair:
            copy.wait_send()

    buffers1 = (sent1, sent1_top, got1, got1_top)
    buffers2 = (sent2, sent2_top, got2, got2_top)
    buffers3 = (sent3, sent3_top, got3, got3_top)
    sems1 = (r1_send, r1_recv, r1t_send, r1t_recv)
    sems2 = (r2_send, r2_recv, r2t_send, r2t_recv)
    sems3 = (r3_send, r3_recv, r3t_send, r3t_recv)

    def large(lane, k, message):
        way = way_of(k)
        return code_copies(lane, (lane, k, message), buffers1, sems1, SCATTER[lane][0],
                           RING - way if message == 1 else way)

    def medium(lane, k):
        return code_copies(lane, (lane, k - 1), buffers2, sems2, SCATTER[lane][1], k)

    def small(lane, k):
        return code_copies(lane, (lane, k - 1), buffers3, sems3, SCATTER[lane][2], k)

    def scatter_large(lane, k, message):
        order = SCATTER[lane]
        way = way_of(k)
        row = on_ring(order[0], (2, RING - way, way)[message])
        middle = on_ring(order[1], k)
        parts = []
        if message == 2:
            landed(large(lane, k, 0))
            parts = [(got1.at[lane, k, 0], got1_top.at[lane, k, 0])]
        encode(lane, lambda at: place(order, row, middle, at), RING, parts,
               sent1.at[lane, k, message], sent1_top.at[lane, k, message])
        begin_all(large(lane, k, message))

    def near_parts(lane, k):
        for message in (1, 2):
            landed(large(lane, k, message))
        return [(got1.at[lane, k, message], got1_top.at[lane, k, message]) for message in (1, 2)]

    def scatter_middle(lane, k):
        order = SCATTER[lane]
        middle = on_ring(order[1], k)
        encode(lane, lambda at: place(order, me[order[0]], middle, at), RING, near_parts(lane, k),
               sent2.at[lane, k - 1], sent2_top.at[lane, k - 1])
        begin_all(medium(lane, k))

    def own_parts(lane):
        parts = near_parts(lane, 0)
        for k in range(1, RING):
            landed(medium(lane, k))
            parts.append((got2.at[lane, k - 1], got2_top.at[lane, k - 1]))
        return parts

    def own_value(lane, parts, at):
        order = SCATTER[lane]
        value = grads[place(order, me[order[0]], me[order[1]], at) + (slice(None), pl.ds(*lanes[lane]))]
        for part in parts:
            value += decoded(part[0], part[1], lane, at)
        return value

    def largest_piece(top):
        pieces = [top[row : row + 8, column : column + 128]
                  for row in range(0, top.shape[0], 8) for column in range(0, top.shape[1], 128)]
        while len(pieces) > 1:
            pieces = [jnp.maximum(*pieces[at : at + 2]) if at + 1 < len(pieces) else pieces[at]
                      for at in range(0, len(pieces), 2)]
        return jnp.maximum(pieces[0], 1e-30)

    def scatter_small(lane, k, parts):
        width = lanes[lane][1]
        value = own_value(lane, parts, on_ring(SCATTER[lane][2], k))
        top = largest_piece(jnp.abs(value))
        sent3_top[lane, k - 1] = top * (1.0 / TOP)
        sent3[lane, k - 1, 0, :, pl.ds(0, width)] = (
            jnp.round(value * spread(TOP / top, width)).astype(jnp.int32).astype(jnp.int16)
        )
        begin_all(small(lane, k))

    def hidden_part(lane, offset):
        axis = GATHER[lane][2]
        columns = pl.ds(*gather_lanes[lane])
        index = tuple(on_ring(axis, offset) if dim == axis else slice(None) for dim in range(3))
        rows = weights[index + (slice(None), columns)].reshape(RING * RING * owned, gather_lanes[lane][1])
        value = lax.dot_general(
            rows, cot[:, columns], (((1,), (1,)), ((), ())), preferred_element_type=jnp.float32
        )
        dh_t[index] = dh_t[index] + value.reshape(RING, RING, owned, tokens)

    limit_mask = lax.broadcasted_iota(jnp.int32, (tokens, 1), 0) < limit
    quarter = RING * RING * owned

    def turn_back(at):
        value = scale * dh_t[at].reshape(quarter, tokens).T
        value = jnp.where(limit_mask, value, 0.0)
        dh[:, pl.ds(pl.multiple_of(at * quarter, quarter), quarter)] = value.astype(dh.dtype)

    every = range(LANES)

    def gather_next(k):
        for slot in range(2):
            for lane in every:
                gather_large(lane, k, slot).start()

    def gather_onward(k):
        for lane in every:
            gather_large(lane, k, 0).wait_recv()
            gather_large(lane, k, 2).start()

    def gather_middle(offset):
        for lane in every:
            gather_small(lane, 1, offset, gb_send, gb_recv).wait_recv()

    load_w.wait()
    for offset in (1, 3, 2):
        for lane in every:
            gather_small(lane, 0, offset, ga_send, ga_recv).start()
    load_hid.wait()
    tiles(tokens // TILE, turn)

    def clear(at):
        dh_t[at] = jnp.zeros(dh_t.shape[1:], jnp.float32)
    tiles(RING, clear)
    for offset in (1, 3, 2):
        for lane in every:
            gather_small(lane, 0, offset, ga_send, ga_recv).wait_recv()
    for offset in (1, 3, 2):
        for lane in every:
            gather_small(lane, 1, offset, gb_send, gb_recv).start()
    gather_next(0)
    load_cot.wait()
    tiles(cot.shape[1] // TILE, product)

    def near_and_far(step):
        k = part_of(step)
        for lane in every:
            scatter_large(lane, k, 0)
            scatter_large(lane, k, 1)
    tiles(RING, near_and_far)
    for offset in (1, 3, 2):
        gather_middle(offset)
    gather_next(1)
    for lane in every:
        hidden_part(lane, 0)

    def with_far(step):
        k = part_of(step)
        for lane in every:
            scatter_large(lane, k, 2)
    tiles(RING, with_far)
    gather_next(3)
    gather_onward(0)

    def second_stage(step):
        k = part_of(step)
        for lane in every:
            scatter_middle(lane, k)
    tiles(RING - 1, second_stage)
    gather_next(2)
    for lane in every:
        parts = own_parts(lane)
        tiles(RING - 1, lambda step, lane=lane, parts=parts: scatter_small(lane, part_of(step), parts))
    gather_onward(1)
    gather_onward(3)
    gather_onward(2)

    for load in (load_mom, load_sec, load_srv):
        load.wait()
    shared = []
    for lane in range(LANES):
        begin, width = lanes[lane]
        columns = pl.ds(begin, width)
        parts = [(got1.at[lane, 0, message], got1_top.at[lane, 0, message]) for message in (1, 2)]
        parts += [(got2.at[lane, slot], got2_top.at[lane, slot]) for slot in range(RING - 1)]
        total = own_value(lane, parts, me[SCATTER[lane][2]])
        for slot in range(RING - 1):
            landed(small(lane, slot + 1))
            total += decoded(got3.at[lane, slot], got3_top.at[lane, slot], lane, 0)
        grad = scale * total
        first_new = beta_one * mom[:, columns] + (1.0 - beta_one) * grad
        squares_new = beta_two * sec[:, columns] + (1.0 - beta_two) * grad * grad
        step = first_new / bias_one / (jnp.sqrt(squares_new / bias_two) + epsilon)
        current = weights[me[0], me[1], me[2], :, columns].astype(jnp.float32)
        updated = current - learn_rate * (step + decay_rate * current)
        delta[core, :, columns] = (updated - current).astype(delta.dtype)
        part = delta.at[core, :, columns]
        shared.append(pltpu.make_async_remote_copy(
            src_ref=part, dst_ref=part, send_sem=d_send.at[lane], recv_sem=d_recv.at[lane],
            device_id={"expert": 1 - core}, device_id_type=MESH,
        ))
        shared[lane].start()
        nw[:, columns] = updated.astype(nw.dtype)
        nm[:, columns] = first_new
        ns[:, columns] = squares_new

    def near_slab(step):
        for lane in every:
            hidden_part(lane, 1 + 2 * step)
    for k in range(RING):
        for lane in every:
            gather_large(lane, k, 1).wait_recv()
    tiles(2, near_slab)
    for lane in range(LANES):
        begin, width = lanes[lane]
        columns = pl.ds(begin, width)
        shared[lane].wait_recv()
        choices = [delta[expert, :, columns].astype(jnp.float32) for expert in range(2)]
        for replica in range(srv.shape[0]):
            pick = jnp.full((owned, width), placement[core, replica], jnp.int32) == 0
            incoming = jnp.where(pick, choices[0], choices[1])
            so[replica, :, columns] = (srv[replica, :, columns].astype(jnp.float32) + incoming).astype(so.dtype)

    def gathered(k):
        for lane in every:
            gather_large(lane, k, 2).wait_recv()
    tiles(RING, gathered)
    for lane in every:
        hidden_part(lane, 2)
    tiles(RING, turn_back)

    def sent_all(k):
        for lane in every:
            for slot in range(3):
                gather_large(lane, k, slot).wait_send()
                gone(large(lane, k, slot))

            @pl.when(k > 0)
            def _():
                gather_small(lane, 0, k, ga_send, ga_recv).wait_send()
                gather_small(lane, 1, k, gb_send, gb_recv).wait_send()
                gone(medium(lane, k))
                gone(small(lane, k))
    tiles(RING, sent_all)
    for copy in shared:
        copy.wait_send()


def store(*refs):
    count = len(refs) // 2
    sem = refs[2 * count]
    copies = [pltpu.make_async_copy(refs[at], refs[count + at], sem.at[at]) for at in range(count)]
    for copy in copies:
        copy.start()
    for copy in copies:
        copy.wait()


def stored(arrays):
    anywhere = pl.BlockSpec(memory_space=pl.ANY)
    return pl.pallas_call(
        store,
        out_shape=tuple(jax.ShapeDtypeStruct(array.shape, array.dtype) for array in arrays),
        in_specs=[anywhere] * len(arrays),
        out_specs=[anywhere] * len(arrays),
        scratch_shapes=[pltpu.SemaphoreType.DMA((len(arrays),))],
        compiler_params=pltpu.CompilerParams(vmem_limit_bytes=2**20),
    )(*arrays)


def on_device(hidden, cotangent, counts, placement, weight, moment, second, serving):
    tokens, rows = hidden.shape[1:]
    width = cotangent.shape[2]
    owned = weight.shape[1]
    copies = serving.shape[1]
    gather_lanes = lane_columns(width, 0)
    lanes = lane_columns(width, 1)
    widest = max(count for _, count in lanes)
    scale = width ** (-0.5)
    anywhere = pl.BlockSpec(memory_space=pl.ANY)
    scalars = pl.BlockSpec(memory_space=pltpu.SMEM)
    f32, bf16, i16 = jnp.float32, jnp.bfloat16, jnp.int16
    dma = pltpu.SemaphoreType.DMA
    outs = pl.pallas_call(
        functools.partial(fused, scale, gather_lanes, lanes),
        out_shape=(
            pltpu.VMEM((tokens, rows), bf16),
            pltpu.VMEM((owned, width), bf16),
            pltpu.VMEM((owned, width), f32),
            pltpu.VMEM((owned, width), f32),
            pltpu.VMEM((copies, owned, width), bf16),
        ),
        in_specs=[scalars, scalars] + [anywhere] * 6,
        out_specs=[pl.BlockSpec(memory_space=pltpu.VMEM)] * 5,
        scratch_shapes=[
            pltpu.VMEM((RING, RING, RING, owned, width), bf16),
            pltpu.VMEM((tokens, rows), bf16),
            pltpu.VMEM((rows, tokens), bf16),
            pltpu.VMEM((tokens, width), bf16),
            pltpu.VMEM((RING, RING, RING, owned, width), f32),
            pltpu.VMEM((RING, RING, RING, owned, tokens), f32),
            pltpu.VMEM((owned, width), f32),
            pltpu.VMEM((owned, width), f32),
            pltpu.VMEM((copies, owned, width), bf16),
            pltpu.VMEM((2, owned, width), bf16),
            pltpu.VMEM((LANES, RING, 3, RING, owned, widest), i16),
            pltpu.VMEM((LANES, RING, 3, RING, owned, widest), i16),
            pltpu.VMEM((LANES, 3, RING, owned, widest), i16),
            pltpu.VMEM((LANES, 3, RING, owned, widest), i16),
            pltpu.VMEM((LANES, 3, 1, owned, widest), i16),
            pltpu.VMEM((LANES, 3, 1, owned, widest), i16),
            pltpu.VMEM((LANES, RING, 3, 8, 128), f32),
            pltpu.VMEM((LANES, RING, 3, 8, 128), f32),
            pltpu.VMEM((LANES, 3, 8, 128), f32),
            pltpu.VMEM((LANES, 3, 8, 128), f32),
            pltpu.VMEM((LANES, 3, 8, 128), f32),
            pltpu.VMEM((LANES, 3, 8, 128), f32),
        ]
        + [dma((LANES, 3))] * 4
        + [dma((LANES, RING, 3))] * 6
        + [dma((LANES, 3))] * 8
        + [dma((LANES,))] * 2
        + [dma((6,))],
        compiler_params=pltpu.CompilerParams(
            collective_id=0, has_side_effects=True, vmem_limit_bytes=56 * 2**20
        ),
        cost_estimate=pl.CostEstimate(flops=4 * tokens * rows * width, bytes_accessed=2**25, transcendentals=0),
    )(counts, placement, hidden[0], cotangent[0], weight[0], moment[0], second[0], serving[0])
    return tuple(out[None] for out in stored(outs))


def solution(mesh):
    torus = Mesh(
        mesh.devices.reshape(RING, RING, RING, mesh.shape["expert"]), ("dp_0", "dp_1", "dp_2", "expert")
    )
    return jax.shard_map(
        on_device,
        mesh=torus,
        in_specs=(
            P("expert", DP, None),
            P("expert", DP, None),
            P("expert", DP),
            P(),
            P("expert", DP, None),
            P("expert", DP, None),
            P("expert", DP, None),
            P("expert", None, DP, None),
        ),
        out_specs=(
            P("expert", DP, None),
            P("expert", DP, None),
            P("expert", DP, None),
            P("expert", DP, None),
            P("expert", None, DP, None),
        ),
        check_vma=False,
    )
```

```python
import functools

import jax
import jax.numpy as jnp
from jax import lax
from jax.experimental import pallas as pl
from jax.experimental.pallas import tpu as pltpu
from jax.sharding import Mesh
from jax.sharding import PartitionSpec as P

DP = ("dp_0", "dp_1", "dp_2")
MESH = pl.DeviceIdType.MESH
RING = 4

beta_one = 0.9
beta_two = 0.95
bias_one = 1.0 - 0.9**20
bias_two = 1.0 - 0.95**20
learn_rate = 0.05
decay_rate = 0.1
epsilon = 1e-08

TILE = 256
TOP = 32000.0
LANES = 3
GATHER = ((2, 1, 0), (0, 2, 1), (1, 0, 2))
SCATTER = ((0, 1, 2), (1, 2, 0), (2, 0, 1))


def lane_columns(width, wider):
    tiles = width // 128
    low = tiles // LANES
    counts = [low] * LANES
    for at in range(tiles - low * LANES):
        counts[(wider + at) % LANES] += 1
    starts = [sum(counts[:lane]) * 128 for lane in range(LANES)]
    return tuple((start, count * 128) for start, count in zip(starts, counts))


def fused(
    scale, gather_lanes, lanes,
    counts, placement, hid_in, cot_in, w_in, mom_in, sec_in, srv_in,
    dh, nw, nm, ns, so,
    weights, hid, hid_t, cot, grads, dh_t, mom, sec, srv, delta,
    sent1, got1, sent2, got2, sent3, got3,
    ga_send, ga_recv, gb_send, gb_recv, gc_send, gc_recv,
    r1_send, r1_recv, r2_send, r2_recv, r3_send, r3_recv,
    d_send, d_recv, in_sem,
):
    me = tuple(lax.axis_index(name) for name in DP)
    core = lax.axis_index("expert")
    tokens = hid.shape[0]
    owned = weights.shape[3]

    def on_ring(axis, offset):
        return lax.rem(me[axis] + (offset + RING) % RING, RING)

    def remote(src, dst, send, recv, axis, offset):
        return pltpu.make_async_remote_copy(
            src_ref=src, dst_ref=dst, send_sem=send, recv_sem=recv,
            device_id={DP[axis]: on_ring(axis, offset)}, device_id_type=MESH,
        )

    def block(at, columns):
        index = tuple(at.get(axis, slice(None)) for axis in range(3))
        return weights.at[index + (slice(None), pl.ds(*columns))]

    barrier = pltpu.get_barrier_semaphore()
    for axis in range(3):
        for offset in range(1, RING):
            pl.semaphore_signal(
                barrier, inc=1, device_id={DP[axis]: on_ring(axis, offset)}, device_id_type=MESH
            )
    pl.semaphore_signal(barrier, inc=1, device_id={"expert": 1 - core}, device_id_type=MESH)

    load_w = pltpu.make_async_copy(w_in, weights.at[me[0], me[1], me[2]], in_sem.at[0])
    load_hid = pltpu.make_async_copy(hid_in, hid, in_sem.at[1])
    load_cot = pltpu.make_async_copy(cot_in, cot, in_sem.at[2])
    load_mom = pltpu.make_async_copy(mom_in, mom, in_sem.at[3])
    load_sec = pltpu.make_async_copy(sec_in, sec, in_sem.at[4])
    load_srv = pltpu.make_async_copy(srv_in, srv, in_sem.at[5])
    for load in (load_w, load_hid, load_cot, load_mom, load_sec, load_srv):
        load.start()

    pl.semaphore_wait(barrier, 3 * (RING - 1) + 1)

    def tiles(count, body):
        def step(at, carry):
            body(at)
            return carry
        lax.fori_loop(0, count, step, 0)

    def part_of(step):
        return jnp.where(step == 0, 2, jnp.where(step == 1, 1, jnp.where(step == 2, 3, 0)))

    def way_of(k):
        return 1 + 2 * lax.rem(k, 2)

    def gather_small(lane, stage, offset, send, recv):
        order = GATHER[lane]
        part = block({axis: me[axis] for axis in order[stage:]}, gather_lanes[lane])
        return remote(part, part, send.at[lane, offset - 1], recv.at[lane, offset - 1], order[stage], offset)

    def gather_large(lane, k, slot):
        _, mid, axis = GATHER[lane]
        way = way_of(k)
        holder = on_ring(axis, -way) if slot == 2 else me[axis]
        part = block({mid: on_ring(mid, k), axis: holder}, gather_lanes[lane])
        offset = RING - way if slot == 1 else way
        return remote(part, part, gc_send.at[lane, k, slot], gc_recv.at[lane, k, slot], axis, offset)

    limit = counts[0, 0]

    def turn(step):
        rows = pl.ds(pl.multiple_of(step * TILE, TILE), TILE)
        slots = lax.broadcasted_iota(jnp.int32, (TILE, 1), 0) + step * TILE
        piece = jnp.where(slots < limit, hid[rows, :].astype(jnp.float32), 0.0)
        hid_t[:, rows] = piece.T.astype(hid_t.dtype)

    def product(at):
        columns = pl.ds(pl.multiple_of(at * TILE, TILE), TILE)
        value = jnp.dot(hid_t[...], cot[:, columns], preferred_element_type=jnp.float32)
        grads[:, :, :, :, columns] = value.reshape(RING, RING, RING, owned, TILE)

    def place(order, first_at, second_at, third_at):
        at = {order[0]: first_at, order[1]: second_at, order[2]: third_at}
        return at[0], at[1], at[2]

    def lane_tiles(lane):
        return lanes[lane][1] // 128

    def exponent_of(largest):
        pieces = [largest[row : row + 8, column : column + 128]
                  for row in range(0, owned, 8) for column in range(0, largest.shape[1], 128)]
        while len(pieces) > 1:
            pieces = [jnp.maximum(*pieces[at : at + 2]) if at + 1 < len(pieces) else pieces[at]
                      for at in range(0, len(pieces), 2)]
        exponent = jnp.ceil(jnp.log2(jnp.maximum(pieces[0], 1e-30)))
        return jnp.concatenate([exponent] * (owned // 8), axis=0)

    def spread(tile, lane):
        return jnp.concatenate([tile] * lane_tiles(lane), axis=1)

    def received(codes, count, lane):
        exponent = codes[count * lane_tiles(lane)].astype(jnp.float32)
        return codes, jnp.exp2(exponent) * (1.0 / TOP)

    def decoded(part, lane, at):
        codes, unit = part
        count = lane_tiles(lane)
        value = jnp.concatenate([codes[at * count + tile] for tile in range(count)], axis=1)
        return value.astype(jnp.float32) * spread(unit, lane)

    def put(codes, lane, at, scaled):
        value = jnp.round(scaled).astype(jnp.int32).astype(jnp.int16)
        for tile in range(lane_tiles(lane)):
            codes[at * lane_tiles(lane) + tile] = value[:, tile * 128 : (tile + 1) * 128]

    def encode(lane, where, count, parts, codes):
        begin, width = lanes[lane]
        columns = pl.ds(begin, width)

        def largest(at, top):
            index = where(at) + (slice(None), columns)
            value = grads[index]
            for part in parts:
                value += decoded(part, lane, at)
            if parts:
                grads[index] = value
            return jnp.maximum(top, jnp.abs(value))
        exponent = exponent_of(lax.fori_loop(0, count, largest, jnp.zeros((owned, width), jnp.float32)))
        codes[count * lane_tiles(lane)] = exponent.astype(jnp.int32).astype(jnp.int16)
        factor = jnp.exp2(-exponent) * TOP

        def code(at):
            put(codes, lane, at, grads[where(at) + (slice(None), columns)] * spread(factor, lane))
        tiles(count, code)

    def code_copy(lane, slot, count, buffers, sems, axis, offset):
        part = slot + (pl.ds(0, count * lane_tiles(lane) + 1),)
        return remote(buffers[0].at[part], buffers[1].at[part], sems[0].at[slot], sems[1].at[slot], axis, offset)

    def large(lane, k, message):
        way = way_of(k)
        return code_copy(lane, (lane, k, message), RING, (sent1, got1), (r1_send, r1_recv), SCATTER[lane][0],
                         RING - way if message == 1 else way)

    def medium(lane, k):
        return code_copy(lane, (lane, k - 1), RING, (sent2, got2), (r2_send, r2_recv), SCATTER[lane][1], k)

    def small(lane, k):
        return code_copy(lane, (lane, k - 1), 1, (sent3, got3), (r3_send, r3_recv), SCATTER[lane][2], k)

    def scatter_large(lane, k, message):
        order = SCATTER[lane]
        way = way_of(k)
        row = on_ring(order[0], (2, RING - way, way)[message])
        middle = on_ring(order[1], k)
        parts = []
        if message == 2:
            large(lane, k, 0).wait_recv()
            parts = [received(got1.at[lane, k, 0], RING, lane)]
        encode(lane, lambda at: place(order, row, middle, at), RING, parts, sent1.at[lane, k, message])
        large(lane, k, message).start()

    def near_parts(lane, k):
        for message in (1, 2):
            large(lane, k, message).wait_recv()
        return [received(got1.at[lane, k, message], RING, lane) for message in (1, 2)]

    def scatter_middle(lane, k):
        order = SCATTER[lane]
        middle = on_ring(order[1], k)
        encode(lane, lambda at: place(order, me[order[0]], middle, at), RING, near_parts(lane, k),
               sent2.at[lane, k - 1])
        medium(lane, k).start()

    def own_parts(lane):
        for k in range(1, RING):
            medium(lane, k).wait_recv()
        return near_parts(lane, 0) + [received(got2.at[lane, slot], RING, lane) for slot in range(RING - 1)]

    def own_value(lane, parts, at):
        order = SCATTER[lane]
        value = grads[place(order, me[order[0]], me[order[1]], at) + (slice(None), pl.ds(*lanes[lane]))]
        for part in parts:
            value += decoded(part, lane, at)
        return value

    def scatter_small(lane, k, parts):
        value = own_value(lane, parts, on_ring(SCATTER[lane][2], k))
        exponent = exponent_of(jnp.abs(value))
        sent3[lane, k - 1, lane_tiles(lane)] = exponent.astype(jnp.int32).astype(jnp.int16)
        put(sent3.at[lane, k - 1], lane, 0, value * spread(jnp.exp2(-exponent) * TOP, lane))
        small(lane, k).start()

    def hidden_part(lane, offset):
        axis = GATHER[lane][2]
        columns = pl.ds(*gather_lanes[lane])
        index = tuple(on_ring(axis, offset) if dim == axis else slice(None) for dim in range(3))
        rows = weights[index + (slice(None), columns)].reshape(RING * RING * owned, gather_lanes[lane][1])
        value = lax.dot_general(
            rows, cot[:, columns], (((1,), (1,)), ((), ())), preferred_element_type=jnp.float32
        )
        dh_t[index] = dh_t[index] + value.reshape(RING, RING, owned, tokens)

    limit_mask = lax.broadcasted_iota(jnp.int32, (tokens, 1), 0) < limit
    quarter = RING * RING * owned

    def turn_back(at):
        value = scale * dh_t[at].reshape(quarter, tokens).T
        value = jnp.where(limit_mask, value, 0.0)
        dh[:, pl.ds(pl.multiple_of(at * quarter, quarter), quarter)] = value.astype(dh.dtype)

    every = range(LANES)

    def gather_next(k):
        for slot in range(2):
            for lane in every:
                gather_large(lane, k, slot).start()

    def gather_onward(k):
        for lane in every:
            gather_large(lane, k, 0).wait_recv()
            gather_large(lane, k, 2).start()

    def gather_middle(offset):
        for lane in every:
            gather_small(lane, 1, offset, gb_send, gb_recv).wait_recv()

    load_w.wait()
    for offset in (1, 3, 2):
        for lane in every:
            gather_small(lane, 0, offset, ga_send, ga_recv).start()
    load_hid.wait()
    tiles(tokens // TILE, turn)

    def clear(at):
        dh_t[at] = jnp.zeros(dh_t.shape[1:], jnp.float32)
    tiles(RING, clear)
    for offset in (1, 3, 2):
        for lane in every:
            gather_small(lane, 0, offset, ga_send, ga_recv).wait_recv()
    for offset in (1, 3, 2):
        for lane in every:
            gather_small(lane, 1, offset, gb_send, gb_recv).start()
    gather_next(0)
    load_cot.wait()
    tiles(cot.shape[1] // TILE, product)

    def near_and_far(step):
        k = part_of(step)
        for lane in every:
            scatter_large(lane, k, 0)
            scatter_large(lane, k, 1)
    gather_middle(3)
    gather_next(1)
    tiles(RING, near_and_far)
    for offset in (1, 2):
        gather_middle(offset)

    def with_far(step):
        k = part_of(step)
        for lane in every:
            scatter_large(lane, k, 2)
    tiles(RING, with_far)
    for lane in every:
        hidden_part(lane, 0)
    gather_onward(0)

    def second_stage(step):
        k = part_of(step)
        for lane in every:
            scatter_middle(lane, k)
    tiles(RING - 1, second_stage)
    gather_next(3)
    gather_next(2)
    for lane in every:
        parts = own_parts(lane)
        tiles(RING - 1, lambda step, lane=lane, parts=parts: scatter_small(lane, part_of(step), parts))
    gather_onward(1)
    gather_onward(3)
    gather_onward(2)

    for load in (load_mom, load_sec, load_srv):
        load.wait()
    shared = []
    for lane in range(LANES):
        begin, width = lanes[lane]
        columns = pl.ds(begin, width)
        parts = [received(got1.at[lane, 0, message], RING, lane) for message in (1, 2)]
        parts += [received(got2.at[lane, slot], RING, lane) for slot in range(RING - 1)]
        total = own_value(lane, parts, me[SCATTER[lane][2]])
        for slot in range(RING - 1):
            small(lane, slot + 1).wait_recv()
            total += decoded(received(got3.at[lane, slot], 1, lane), lane, 0)
        grad = scale * total
        first_new = beta_one * mom[:, columns] + (1.0 - beta_one) * grad
        squares_new = beta_two * sec[:, columns] + (1.0 - beta_two) * grad * grad
        step = first_new / bias_one / (jnp.sqrt(squares_new / bias_two) + epsilon)
        current = weights[me[0], me[1], me[2], :, columns].astype(jnp.float32)
        updated = current - learn_rate * (step + decay_rate * current)
        delta[core, :, columns] = (updated - current).astype(delta.dtype)
        part = delta.at[core, :, columns]
        shared.append(pltpu.make_async_remote_copy(
            src_ref=part, dst_ref=part, send_sem=d_send.at[lane], recv_sem=d_recv.at[lane],
            device_id={"expert": 1 - core}, device_id_type=MESH,
        ))
        shared[lane].start()
        nw[:, columns] = updated.astype(nw.dtype)
        nm[:, columns] = first_new
        ns[:, columns] = squares_new

    def near_slab(step):
        for lane in every:
            hidden_part(lane, 1 + 2 * step)
    for k in range(RING):
        for lane in every:
            gather_large(lane, k, 1).wait_recv()
    tiles(2, near_slab)
    for lane in range(LANES):
        begin, width = lanes[lane]
        columns = pl.ds(begin, width)
        shared[lane].wait_recv()
        choices = [delta[expert, :, columns].astype(jnp.float32) for expert in range(2)]
        for replica in range(srv.shape[0]):
            pick = jnp.full((owned, width), placement[core, replica], jnp.int32) == 0
            incoming = jnp.where(pick, choices[0], choices[1])
            so[replica, :, columns] = (srv[replica, :, columns].astype(jnp.float32) + incoming).astype(so.dtype)

    def sent_all(k):
        for lane in every:
            for slot in range(2):
                gather_large(lane, k, slot).wait_send()
            for slot in range(3):
                large(lane, k, slot).wait_send()

            @pl.when(k > 0)
            def _():
                gather_small(lane, 0, k, ga_send, ga_recv).wait_send()
                gather_small(lane, 1, k, gb_send, gb_recv).wait_send()
                medium(lane, k).wait_send()
                small(lane, k).wait_send()
    tiles(RING, sent_all)
    for copy in shared:
        copy.wait_send()

    def gathered(k):
        for lane in every:
            gather_large(lane, k, 2).wait()
    tiles(RING, gathered)
    for lane in every:
        hidden_part(lane, 2)
    tiles(RING, turn_back)


def store(*refs):
    count = len(refs) // 2
    sem = refs[2 * count]
    copies = [pltpu.make_async_copy(refs[at], refs[count + at], sem.at[at]) for at in range(count)]
    for copy in copies:
        copy.start()
    for copy in copies:
        copy.wait()


def stored(arrays):
    anywhere = pl.BlockSpec(memory_space=pl.ANY)
    return pl.pallas_call(
        store,
        out_shape=tuple(jax.ShapeDtypeStruct(array.shape, array.dtype) for array in arrays),
        in_specs=[anywhere] * len(arrays),
        out_specs=[anywhere] * len(arrays),
        scratch_shapes=[pltpu.SemaphoreType.DMA((len(arrays),))],
        compiler_params=pltpu.CompilerParams(vmem_limit_bytes=2**20),
    )(*arrays)


def on_device(hidden, cotangent, counts, placement, weight, moment, second, serving):
    tokens, rows = hidden.shape[1:]
    width = cotangent.shape[2]
    owned = weight.shape[1]
    copies = serving.shape[1]
    gather_lanes = lane_columns(width, 0)
    lanes = lane_columns(width, 1)
    most = max(count for _, count in lanes) // 128
    scale = width ** (-0.5)
    anywhere = pl.BlockSpec(memory_space=pl.ANY)
    scalars = pl.BlockSpec(memory_space=pltpu.SMEM)
    f32, bf16, i16 = jnp.float32, jnp.bfloat16, jnp.int16
    dma = pltpu.SemaphoreType.DMA
    outs = pl.pallas_call(
        functools.partial(fused, scale, gather_lanes, lanes),
        out_shape=(
            pltpu.VMEM((tokens, rows), bf16),
            pltpu.VMEM((owned, width), bf16),
            pltpu.VMEM((owned, width), f32),
            pltpu.VMEM((owned, width), f32),
            pltpu.VMEM((copies, owned, width), bf16),
        ),
        in_specs=[scalars, scalars] + [anywhere] * 6,
        out_specs=[pl.BlockSpec(memory_space=pltpu.VMEM)] * 5,
        scratch_shapes=[
            pltpu.VMEM((RING, RING, RING, owned, width), bf16),
            pltpu.VMEM((tokens, rows), bf16),
            pltpu.VMEM((rows, tokens), bf16),
            pltpu.VMEM((tokens, width), bf16),
            pltpu.VMEM((RING, RING, RING, owned, width), f32),
            pltpu.VMEM((RING, RING, RING, owned, tokens), f32),
            pltpu.VMEM((owned, width), f32),
            pltpu.VMEM((owned, width), f32),
            pltpu.VMEM((copies, owned, width), bf16),
            pltpu.VMEM((2, owned, width), bf16),
            pltpu.VMEM((LANES, RING, 3, RING * most + 1, owned, 128), i16),
            pltpu.VMEM((LANES, RING, 3, RING * most + 1, owned, 128), i16),
            pltpu.VMEM((LANES, 3, RING * most + 1, owned, 128), i16),
            pltpu.VMEM((LANES, 3, RING * most + 1, owned, 128), i16),
            pltpu.VMEM((LANES, 3, most + 1, owned, 128), i16),
            pltpu.VMEM((LANES, 3, most + 1, owned, 128), i16),
        ]
        + [dma((LANES, 3))] * 4
        + [dma((LANES, RING, 3))] * 4
        + [dma((LANES, 3))] * 4
        + [dma((LANES,))] * 2
        + [dma((6,))],
        compiler_params=pltpu.CompilerParams(
            collective_id=0, has_side_effects=True, vmem_limit_bytes=56 * 2**20
        ),
        cost_estimate=pl.CostEstimate(flops=4 * tokens * rows * width, bytes_accessed=2**25, transcendentals=0),
    )(counts, placement, hidden[0], cotangent[0], weight[0], moment[0], second[0], serving[0])
    return tuple(out[None] for out in stored(outs))


def solution(mesh):
    torus = Mesh(
        mesh.devices.reshape(RING, RING, RING, mesh.shape["expert"]), ("dp_0", "dp_1", "dp_2", "expert")
    )
    return jax.shard_map(
        on_device,
        mesh=torus,
        in_specs=(
            P("expert", DP, None),
            P("expert", DP, None),
            P("expert", DP),
            P(),
            P("expert", DP, None),
            P("expert", DP, None),
            P("expert", DP, None),
            P("expert", None, DP, None),
        ),
        out_specs=(
            P("expert", DP, None),
            P("expert", DP, None),
            P("expert", DP, None),
            P("expert", DP, None),
            P("expert", None, DP, None),
        ),
        check_vma=False,
    )
```

```python
import functools

import jax
import jax.numpy as jnp
from jax import lax
from jax.experimental import pallas as pl
from jax.experimental.pallas import tpu as pltpu
from jax.sharding import Mesh
from jax.sharding import PartitionSpec as P

DP = ("dp_0", "dp_1", "dp_2")
MESH = pl.DeviceIdType.MESH
RING = 4

beta_one = 0.9
beta_two = 0.95
bias_one = 1.0 - 0.9**20
bias_two = 1.0 - 0.95**20
learn_rate = 0.05
decay_rate = 0.1
epsilon = 1e-08

TILE = 256
TOP = 32000.0
LANES = 3
GATHER = ((2, 1, 0), (0, 2, 1), (1, 0, 2))
SCATTER = ((0, 1, 2), (1, 2, 0), (2, 0, 1))


def lane_columns(width, wider):
    tiles = width // 128
    low = tiles // LANES
    counts = [low] * LANES
    for at in range(tiles - low * LANES):
        counts[(wider + at) % LANES] += 1
    starts = [sum(counts[:lane]) * 128 for lane in range(LANES)]
    return tuple((start, count * 128) for start, count in zip(starts, counts))


def fused(
    scale, gather_lanes, lanes,
    counts, placement, hid_in, cot_in, w_in, mom_in, sec_in, srv_in,
    dh, nw, nm, ns, so,
    weights, hid, hid_t, cot, grads, dh_t, mom, sec, srv, delta,
    sent1, got1, sent2, got2, sent3, got3,
    ga_send, ga_recv, gb_send, gb_recv, gc_send, gc_recv,
    r1_send, r1_recv, r2_send, r2_recv, r3_send, r3_recv,
    d_send, d_recv, in_sem,
):
    me = tuple(lax.axis_index(name) for name in DP)
    core = lax.axis_index("expert")
    tokens = hid.shape[0]
    owned = weights.shape[3]

    def on_ring(axis, offset):
        return lax.rem(me[axis] + (offset + RING) % RING, RING)

    def remote(src, dst, send, recv, axis, offset):
        return pltpu.make_async_remote_copy(
            src_ref=src, dst_ref=dst, send_sem=send, recv_sem=recv,
            device_id={DP[axis]: on_ring(axis, offset)}, device_id_type=MESH,
        )

    def block(at, columns):
        index = tuple(at.get(axis, slice(None)) for axis in range(3))
        return weights.at[index + (slice(None), pl.ds(*columns))]

    barrier = pltpu.get_barrier_semaphore()
    for axis in range(3):
        for offset in range(1, RING):
            pl.semaphore_signal(
                barrier, inc=1, device_id={DP[axis]: on_ring(axis, offset)}, device_id_type=MESH
            )
    pl.semaphore_signal(barrier, inc=1, device_id={"expert": 1 - core}, device_id_type=MESH)

    load_w = pltpu.make_async_copy(w_in, weights.at[me[0], me[1], me[2]], in_sem.at[0])
    load_hid = pltpu.make_async_copy(hid_in, hid, in_sem.at[1])
    load_cot = pltpu.make_async_copy(cot_in, cot, in_sem.at[2])
    load_mom = pltpu.make_async_copy(mom_in, mom, in_sem.at[3])
    load_sec = pltpu.make_async_copy(sec_in, sec, in_sem.at[4])
    load_srv = pltpu.make_async_copy(srv_in, srv, in_sem.at[5])
    for load in (load_w, load_hid, load_cot, load_mom, load_sec, load_srv):
        load.start()

    pl.semaphore_wait(barrier, 3 * (RING - 1) + 1)

    def tiles(count, body):
        def step(at, carry):
            body(at)
            return carry
        lax.fori_loop(0, count, step, 0)

    def part_of(step):
        return jnp.where(step == 0, 2, jnp.where(step == 1, 1, jnp.where(step == 2, 3, 0)))

    def way_of(k):
        return 1 + 2 * lax.rem(k, 2)

    def gather_small(lane, stage, offset, send, recv):
        order = GATHER[lane]
        part = block({axis: me[axis] for axis in order[stage:]}, gather_lanes[lane])
        return remote(part, part, send.at[lane, offset - 1], recv.at[lane, offset - 1], order[stage], offset)

    def gather_half(lane, half):
        first, mid, axis = GATHER[lane]
        way = (1, 3)[half]
        part = block({first: pl.ds(2 * half, 2), mid: on_ring(mid, -way), axis: me[axis]}, gather_lanes[lane])
        return remote(part, part, gb_send.at[lane, 1 + 2 * half], gb_recv.at[lane, 1 + 2 * half], mid, way)

    def gather_large(lane, k, slot):
        _, mid, axis = GATHER[lane]
        way = way_of(k)
        holder = on_ring(axis, -way) if slot == 2 else me[axis]
        part = block({mid: on_ring(mid, k), axis: holder}, gather_lanes[lane])
        offset = RING - way if slot == 1 else way
        return remote(part, part, gc_send.at[lane, k, slot], gc_recv.at[lane, k, slot], axis, offset)

    def gather_halves():
        for half, offset in enumerate((1, 3)):
            for lane in range(LANES):
                gather_small(lane, 1, offset, gb_send, gb_recv).wait_recv()
            for lane in range(LANES):
                gather_half(lane, half).start()

    limit = counts[0, 0]

    def turn(step):
        rows = pl.ds(pl.multiple_of(step * TILE, TILE), TILE)
        slots = lax.broadcasted_iota(jnp.int32, (TILE, 1), 0) + step * TILE
        piece = jnp.where(slots < limit, hid[rows, :].astype(jnp.float32), 0.0)
        hid_t[:, rows] = piece.T.astype(hid_t.dtype)

    def product(at):
        columns = pl.ds(pl.multiple_of(at * TILE, TILE), TILE)
        value = jnp.dot(hid_t[...], cot[:, columns], preferred_element_type=jnp.float32)
        grads[:, :, :, :, columns] = value.reshape(RING, RING, RING, owned, TILE)

    def place(order, first_at, second_at, third_at):
        at = {order[0]: first_at, order[1]: second_at, order[2]: third_at}
        return at[0], at[1], at[2]

    def lane_tiles(lane):
        return lanes[lane][1] // 128

    def exponent_of(largest):
        pieces = [largest[row : row + 8, column : column + 128]
                  for row in range(0, owned, 8) for column in range(0, largest.shape[1], 128)]
        while len(pieces) > 1:
            pieces = [jnp.maximum(*pieces[at : at + 2]) if at + 1 < len(pieces) else pieces[at]
                      for at in range(0, len(pieces), 2)]
        exponent = jnp.ceil(jnp.log2(jnp.maximum(pieces[0], 1e-30)))
        return jnp.concatenate([exponent] * (owned // 8), axis=0)

    def spread(tile, lane):
        return jnp.concatenate([tile] * lane_tiles(lane), axis=1)

    def received(codes, count, lane):
        exponent = codes[count * lane_tiles(lane)].astype(jnp.float32)
        return codes, jnp.exp2(exponent) * (1.0 / TOP)

    def decoded(part, lane, at):
        codes, unit = part
        count = lane_tiles(lane)
        value = jnp.concatenate([codes[at * count + tile] for tile in range(count)], axis=1)
        return value.astype(jnp.float32) * spread(unit, lane)

    def put(codes, lane, at, scaled):
        value = jnp.round(scaled).astype(jnp.int32).astype(jnp.int16)
        for tile in range(lane_tiles(lane)):
            codes[at * lane_tiles(lane) + tile] = value[:, tile * 128 : (tile + 1) * 128]

    def encode(lane, where, count, parts, codes):
        begin, width = lanes[lane]
        columns = pl.ds(begin, width)

        def largest(at, top):
            index = where(at) + (slice(None), columns)
            value = grads[index]
            for part in parts:
                value += decoded(part, lane, at)
            if parts:
                grads[index] = value
            return jnp.maximum(top, jnp.abs(value))
        exponent = exponent_of(lax.fori_loop(0, count, largest, jnp.zeros((owned, width), jnp.float32)))
        codes[count * lane_tiles(lane)] = exponent.astype(jnp.int32).astype(jnp.int16)
        factor = jnp.exp2(-exponent) * TOP

        def code(at):
            put(codes, lane, at, grads[where(at) + (slice(None), columns)] * spread(factor, lane))
        tiles(count, code)

    def code_copy(lane, slot, count, buffers, sems, axis, offset):
        part = slot + (pl.ds(0, count * lane_tiles(lane) + 1),)
        return remote(buffers[0].at[part], buffers[1].at[part], sems[0].at[slot], sems[1].at[slot], axis, offset)

    def large(lane, k, message):
        way = way_of(k)
        return code_copy(lane, (lane, k, message), RING, (sent1, got1), (r1_send, r1_recv), SCATTER[lane][0],
                         RING - way if message == 1 else way)

    def medium(lane, k):
        return code_copy(lane, (lane, k - 1), RING, (sent2, got2), (r2_send, r2_recv), SCATTER[lane][1], k)

    def small(lane, k):
        return code_copy(lane, (lane, k - 1), 1, (sent3, got3), (r3_send, r3_recv), SCATTER[lane][2], k)

    def scatter_large(lane, k, message):
        order = SCATTER[lane]
        way = way_of(k)
        row = on_ring(order[0], (2, RING - way, way)[message])
        middle = on_ring(order[1], k)
        parts = []
        if message == 2:
            large(lane, k, 0).wait_recv()
            parts = [received(got1.at[lane, k, 0], RING, lane)]
        encode(lane, lambda at: place(order, row, middle, at), RING, parts, sent1.at[lane, k, message])
        large(lane, k, message).start()

    def near_parts(lane, k):
        for message in (1, 2):
            large(lane, k, message).wait_recv()
        return [received(got1.at[lane, k, message], RING, lane) for message in (1, 2)]

    def scatter_middle(lane, k):
        order = SCATTER[lane]
        middle = on_ring(order[1], k)
        encode(lane, lambda at: place(order, me[order[0]], middle, at), RING, near_parts(lane, k),
               sent2.at[lane, k - 1])
        medium(lane, k).start()

    def own_parts(lane):
        for k in range(1, RING):
            medium(lane, k).wait_recv()
        return near_parts(lane, 0) + [received(got2.at[lane, slot], RING, lane) for slot in range(RING - 1)]

    def own_value(lane, parts, at):
        order = SCATTER[lane]
        value = grads[place(order, me[order[0]], me[order[1]], at) + (slice(None), pl.ds(*lanes[lane]))]
        for part in parts:
            value += decoded(part, lane, at)
        return value

    def scatter_small(lane, k, parts):
        value = own_value(lane, parts, on_ring(SCATTER[lane][2], k))
        exponent = exponent_of(jnp.abs(value))
        sent3[lane, k - 1, lane_tiles(lane)] = exponent.astype(jnp.int32).astype(jnp.int16)
        put(sent3.at[lane, k - 1], lane, 0, value * spread(jnp.exp2(-exponent) * TOP, lane))
        small(lane, k).start()

    def hidden_part(lane, offset):
        axis = GATHER[lane][2]
        columns = pl.ds(*gather_lanes[lane])
        index = tuple(on_ring(axis, offset) if dim == axis else slice(None) for dim in range(3))
        rows = weights[index + (slice(None), columns)].reshape(RING * RING * owned, gather_lanes[lane][1])
        value = lax.dot_general(
            rows, cot[:, columns], (((1,), (1,)), ((), ())), preferred_element_type=jnp.float32
        )
        dh_t[index] = dh_t[index] + value.reshape(RING, RING, owned, tokens)

    limit_mask = lax.broadcasted_iota(jnp.int32, (tokens, 1), 0) < limit
    quarter = RING * RING * owned

    def turn_back(at):
        value = scale * dh_t[at].reshape(quarter, tokens).T
        value = jnp.where(limit_mask, value, 0.0)
        dh[:, pl.ds(pl.multiple_of(at * quarter, quarter), quarter)] = value.astype(dh.dtype)

    every = range(LANES)

    def gather_next(k):
        for slot in range(2):
            for lane in every:
                gather_large(lane, k, slot).start()

    def gather_onward(k):
        for lane in every:
            gather_large(lane, k, 0).wait_recv()
            gather_large(lane, k, 2).start()

    load_w.wait()
    for offset in (1, 3, 2):
        for lane in every:
            gather_small(lane, 0, offset, ga_send, ga_recv).start()
    load_hid.wait()
    tiles(tokens // TILE, turn)

    def clear(at):
        dh_t[at] = jnp.zeros(dh_t.shape[1:], jnp.float32)
    tiles(RING, clear)
    for offset in (1, 3, 2):
        for lane in every:
            gather_small(lane, 0, offset, ga_send, ga_recv).wait_recv()
    for offset in (1, 3):
        for lane in every:
            gather_small(lane, 1, offset, gb_send, gb_recv).start()
    gather_next(0)
    load_cot.wait()

    def product_step(at):
        product(at)

        @pl.when(at == 5)
        def _():
            gather_halves()
            gather_next(1)
    tiles(cot.shape[1] // TILE, product_step)

    def near_and_far(step):
        k = part_of(step)
        for lane in every:
            scatter_large(lane, k, 0)
            scatter_large(lane, k, 1)
    tiles(RING, near_and_far)
    for lane in every:
        gather_half(lane, 0).wait_recv()
        gather_half(lane, 1).wait_recv()

    def with_far(step):
        k = part_of(step)
        for lane in every:
            scatter_large(lane, k, 2)
    tiles(RING, with_far)
    for lane in every:
        hidden_part(lane, 0)
    gather_onward(0)

    def second_stage(step):
        k = part_of(step)
        for lane in every:
            scatter_middle(lane, k)
    tiles(RING - 1, second_stage)
    gather_next(3)
    gather_next(2)
    for lane in every:
        parts = own_parts(lane)
        tiles(RING - 1, lambda step, lane=lane, parts=parts: scatter_small(lane, part_of(step), parts))
    gather_onward(1)
    gather_onward(3)
    gather_onward(2)

    for load in (load_mom, load_sec, load_srv):
        load.wait()
    shared = []
    for lane in range(LANES):
        begin, width = lanes[lane]
        columns = pl.ds(begin, width)
        parts = [received(got1.at[lane, 0, message], RING, lane) for message in (1, 2)]
        parts += [received(got2.at[lane, slot], RING, lane) for slot in range(RING - 1)]
        total = own_value(lane, parts, me[SCATTER[lane][2]])
        for slot in range(RING - 1):
            small(lane, slot + 1).wait_recv()
            total += decoded(received(got3.at[lane, slot], 1, lane), lane, 0)
        grad = scale * total
        first_new = beta_one * mom[:, columns] + (1.0 - beta_one) * grad
        squares_new = beta_two * sec[:, columns] + (1.0 - beta_two) * grad * grad
        step = first_new / bias_one / (jnp.sqrt(squares_new / bias_two) + epsilon)
        current = weights[me[0], me[1], me[2], :, columns].astype(jnp.float32)
        updated = current - learn_rate * (step + decay_rate * current)
        delta[core, :, columns] = (updated - current).astype(delta.dtype)
        part = delta.at[core, :, columns]
        shared.append(pltpu.make_async_remote_copy(
            src_ref=part, dst_ref=part, send_sem=d_send.at[lane], recv_sem=d_recv.at[lane],
            device_id={"expert": 1 - core}, device_id_type=MESH,
        ))
        shared[lane].start()
        nw[:, columns] = updated.astype(nw.dtype)
        nm[:, columns] = first_new
        ns[:, columns] = squares_new

    def near_slab(step):
        for lane in every:
            hidden_part(lane, 1 + 2 * step)
    for k in range(RING):
        for lane in every:
            gather_large(lane, k, 1).wait_recv()
    tiles(2, near_slab)
    for lane in range(LANES):
        begin, width = lanes[lane]
        columns = pl.ds(begin, width)
        shared[lane].wait_recv()
        choices = [delta[expert, :, columns].astype(jnp.float32) for expert in range(2)]
        for replica in range(srv.shape[0]):
            pick = jnp.full((owned, width), placement[core, replica], jnp.int32) == 0
            incoming = jnp.where(pick, choices[0], choices[1])
            so[replica, :, columns] = (srv[replica, :, columns].astype(jnp.float32) + incoming).astype(so.dtype)

    def sent_all(k):
        for lane in every:
            for slot in range(2):
                gather_large(lane, k, slot).wait_send()
            for slot in range(3):
                large(lane, k, slot).wait_send()

            @pl.when(k > 0)
            def _():
                gather_small(lane, 0, k, ga_send, ga_recv).wait_send()
                medium(lane, k).wait_send()
                small(lane, k).wait_send()
    tiles(RING, sent_all)
    for lane in every:
        for half, offset in enumerate((1, 3)):
            gather_small(lane, 1, offset, gb_send, gb_recv).wait_send()
            gather_half(lane, half).wait_send()
    for copy in shared:
        copy.wait_send()

    def gathered(k):
        for lane in every:
            gather_large(lane, k, 2).wait()
    tiles(RING, gathered)
    for lane in every:
        hidden_part(lane, 2)
    tiles(RING, turn_back)


def store(*refs):
    count = len(refs) // 2
    sem = refs[2 * count]
    copies = [pltpu.make_async_copy(refs[at], refs[count + at], sem.at[at]) for at in range(count)]
    for copy in copies:
        copy.start()
    for copy in copies:
        copy.wait()


def stored(arrays):
    anywhere = pl.BlockSpec(memory_space=pl.ANY)
    return pl.pallas_call(
        store,
        out_shape=tuple(jax.ShapeDtypeStruct(array.shape, array.dtype) for array in arrays),
        in_specs=[anywhere] * len(arrays),
        out_specs=[anywhere] * len(arrays),
        scratch_shapes=[pltpu.SemaphoreType.DMA((len(arrays),))],
        compiler_params=pltpu.CompilerParams(vmem_limit_bytes=2**20),
    )(*arrays)


def on_device(hidden, cotangent, counts, placement, weight, moment, second, serving):
    tokens, rows = hidden.shape[1:]
    width = cotangent.shape[2]
    owned = weight.shape[1]
    copies = serving.shape[1]
    gather_lanes = lane_columns(width, 0)
    lanes = lane_columns(width, 1)
    most = max(count for _, count in lanes) // 128
    scale = width ** (-0.5)
    anywhere = pl.BlockSpec(memory_space=pl.ANY)
    scalars = pl.BlockSpec(memory_space=pltpu.SMEM)
    f32, bf16, i16 = jnp.float32, jnp.bfloat16, jnp.int16
    dma = pltpu.SemaphoreType.DMA
    outs = pl.pallas_call(
        functools.partial(fused, scale, gather_lanes, lanes),
        out_shape=(
            pltpu.VMEM((tokens, rows), bf16),
            pltpu.VMEM((owned, width), bf16),
            pltpu.VMEM((owned, width), f32),
            pltpu.VMEM((owned, width), f32),
            pltpu.VMEM((copies, owned, width), bf16),
        ),
        in_specs=[scalars, scalars] + [anywhere] * 6,
        out_specs=[pl.BlockSpec(memory_space=pltpu.VMEM)] * 5,
        scratch_shapes=[
            pltpu.VMEM((RING, RING, RING, owned, width), bf16),
            pltpu.VMEM((tokens, rows), bf16),
            pltpu.VMEM((rows, tokens), bf16),
            pltpu.VMEM((tokens, width), bf16),
            pltpu.VMEM((RING, RING, RING, owned, width), f32),
            pltpu.VMEM((RING, RING, RING, owned, tokens), f32),
            pltpu.VMEM((owned, width), f32),
            pltpu.VMEM((owned, width), f32),
            pltpu.VMEM((copies, owned, width), bf16),
            pltpu.VMEM((2, owned, width), bf16),
            pltpu.VMEM((LANES, RING, 3, RING * most + 1, owned, 128), i16),
            pltpu.VMEM((LANES, RING, 3, RING * most + 1, owned, 128), i16),
            pltpu.VMEM((LANES, 3, RING * most + 1, owned, 128), i16),
            pltpu.VMEM((LANES, 3, RING * most + 1, owned, 128), i16),
            pltpu.VMEM((LANES, 3, most + 1, owned, 128), i16),
            pltpu.VMEM((LANES, 3, most + 1, owned, 128), i16),
        ]
        + [dma((LANES, 3))] * 2
        + [dma((LANES, RING))] * 2
        + [dma((LANES, RING, 3))] * 4
        + [dma((LANES, 3))] * 4
        + [dma((LANES,))] * 2
        + [dma((6,))],
        compiler_params=pltpu.CompilerParams(
            collective_id=0, has_side_effects=True, vmem_limit_bytes=56 * 2**20
        ),
        cost_estimate=pl.CostEstimate(flops=4 * tokens * rows * width, bytes_accessed=2**25, transcendentals=0),
    )(counts, placement, hidden[0], cotangent[0], weight[0], moment[0], second[0], serving[0])
    return tuple(out[None] for out in stored(outs))


def solution(mesh):
    torus = Mesh(
        mesh.devices.reshape(RING, RING, RING, mesh.shape["expert"]), ("dp_0", "dp_1", "dp_2", "expert")
    )
    return jax.shard_map(
        on_device,
        mesh=torus,
        in_specs=(
            P("expert", DP, None),
            P("expert", DP, None),
            P("expert", DP),
            P(),
            P("expert", DP, None),
            P("expert", DP, None),
            P("expert", DP, None),
            P("expert", None, DP, None),
        ),
        out_specs=(
            P("expert", DP, None),
            P("expert", DP, None),
            P("expert", DP, None),
            P("expert", DP, None),
            P("expert", None, DP, None),
        ),
        check_vma=False,
    )
```

```python
import functools

import jax
import jax.numpy as jnp
from jax import lax
from jax.experimental import pallas as pl
from jax.experimental.pallas import tpu as pltpu
from jax.sharding import Mesh
from jax.sharding import PartitionSpec as P

DP = ("dp_0", "dp_1", "dp_2")
MESH = pl.DeviceIdType.MESH
RING = 4

beta_one = 0.9
beta_two = 0.95
bias_one = 1.0 - 0.9**20
bias_two = 1.0 - 0.95**20
learn_rate = 0.05
decay_rate = 0.1
epsilon = 1e-08

TILE = 256
TOP = 32000.0
LANES = 3
GATHER = ((2, 1, 0), (0, 2, 1), (1, 0, 2))
SCATTER = ((0, 1, 2), (1, 2, 0), (2, 0, 1))


def lane_columns(width, wider):
    tiles = width // 128
    low = tiles // LANES
    counts = [low] * LANES
    for at in range(tiles - low * LANES):
        counts[(wider + at) % LANES] += 1
    starts = [sum(counts[:lane]) * 128 for lane in range(LANES)]
    return tuple((start, count * 128) for start, count in zip(starts, counts))


def fused(
    scale, gather_lanes, lanes,
    counts, placement, hid_in, cot_in, w_in, mom_in, sec_in, srv_in,
    dh, nw, nm, ns, so,
    weights, hid, hid_t, cot, grads, dh_t, mom, sec, srv, delta,
    sent1, got1, sent2, got2, sent3, got3,
    ga_send, ga_recv, gb_send, gb_recv, gc_send, gc_recv,
    r1_send, r1_recv, r2_send, r2_recv, r3_send, r3_recv,
    d_send, d_recv, in_sem,
):
    me = tuple(lax.axis_index(name) for name in DP)
    core = lax.axis_index("expert")
    tokens = hid.shape[0]
    owned = weights.shape[3]

    def on_ring(axis, offset):
        return lax.rem(me[axis] + (offset + RING) % RING, RING)

    def remote(src, dst, send, recv, axis, offset):
        return pltpu.make_async_remote_copy(
            src_ref=src, dst_ref=dst, send_sem=send, recv_sem=recv,
            device_id={DP[axis]: on_ring(axis, offset)}, device_id_type=MESH,
        )

    def block(at, columns):
        index = tuple(at.get(axis, slice(None)) for axis in range(3))
        return weights.at[index + (slice(None), pl.ds(*columns))]

    barrier = pltpu.get_barrier_semaphore()
    for axis in range(3):
        for offset in range(1, RING):
            pl.semaphore_signal(
                barrier, inc=1, device_id={DP[axis]: on_ring(axis, offset)}, device_id_type=MESH
            )
    pl.semaphore_signal(barrier, inc=1, device_id={"expert": 1 - core}, device_id_type=MESH)

    load_w = pltpu.make_async_copy(w_in, weights.at[me[0], me[1], me[2]], in_sem.at[0])
    load_hid = pltpu.make_async_copy(hid_in, hid, in_sem.at[1])
    load_cot = pltpu.make_async_copy(cot_in, cot, in_sem.at[2])
    load_mom = pltpu.make_async_copy(mom_in, mom, in_sem.at[3])
    load_sec = pltpu.make_async_copy(sec_in, sec, in_sem.at[4])
    load_srv = pltpu.make_async_copy(srv_in, srv, in_sem.at[5])
    for load in (load_w, load_hid, load_cot, load_mom, load_sec, load_srv):
        load.start()

    pl.semaphore_wait(barrier, 3 * (RING - 1) + 1)

    def tiles(count, body):
        def step(at, carry):
            body(at)
            return carry
        lax.fori_loop(0, count, step, 0)

    def part_of(step):
        return jnp.where(step == 0, 2, jnp.where(step == 1, 1, jnp.where(step == 2, 3, 0)))

    def way_of(k):
        return 1 + 2 * lax.rem(k, 2)

    def gather_small(lane, stage, offset, send, recv):
        order = GATHER[lane]
        part = block({axis: me[axis] for axis in order[stage:]}, gather_lanes[lane])
        return remote(part, part, send.at[lane, offset - 1], recv.at[lane, offset - 1], order[stage], offset)

    def gather_half(lane, half):
        first, mid, axis = GATHER[lane]
        way = (1, 3)[half]
        part = block({first: pl.ds(2 * half, 2), mid: on_ring(mid, -way), axis: me[axis]}, gather_lanes[lane])
        return remote(part, part, gb_send.at[lane, 1 + 2 * half], gb_recv.at[lane, 1 + 2 * half], mid, way)

    def gather_large(lane, k, slot):
        _, mid, axis = GATHER[lane]
        way = way_of(k)
        holder = on_ring(axis, -way) if slot == 2 else me[axis]
        part = block({mid: on_ring(mid, k), axis: holder}, gather_lanes[lane])
        offset = RING - way if slot == 1 else way
        return remote(part, part, gc_send.at[lane, k, slot], gc_recv.at[lane, k, slot], axis, offset)

    def gather_halves():
        for half, offset in enumerate((1, 3)):
            for lane in range(LANES):
                gather_small(lane, 1, offset, gb_send, gb_recv).wait_recv()
            for lane in range(LANES):
                gather_half(lane, half).start()

    limit = counts[0, 0]

    def turn(step):
        rows = pl.ds(pl.multiple_of(step * TILE, TILE), TILE)
        slots = lax.broadcasted_iota(jnp.int32, (TILE, 1), 0) + step * TILE
        piece = jnp.where(slots < limit, hid[rows, :].astype(jnp.float32), 0.0)
        hid_t[:, rows] = piece.T.astype(hid_t.dtype)

    def product(at):
        columns = pl.ds(pl.multiple_of(at * TILE, TILE), TILE)
        value = jnp.dot(hid_t[...], cot[:, columns], preferred_element_type=jnp.float32)
        grads[:, :, :, :, columns] = value.reshape(RING, RING, RING, owned, TILE)

    def place(order, first_at, second_at, third_at):
        at = {order[0]: first_at, order[1]: second_at, order[2]: third_at}
        return at[0], at[1], at[2]

    def lane_tiles(lane):
        return lanes[lane][1] // 128

    def exponent_of(largest):
        pieces = [largest[row : row + 8, column : column + 128]
                  for row in range(0, owned, 8) for column in range(0, largest.shape[1], 128)]
        while len(pieces) > 1:
            pieces = [jnp.maximum(*pieces[at : at + 2]) if at + 1 < len(pieces) else pieces[at]
                      for at in range(0, len(pieces), 2)]
        exponent = jnp.ceil(jnp.log2(jnp.maximum(pieces[0], 1e-30)))
        return jnp.concatenate([exponent] * (owned // 8), axis=0)

    def spread(tile, lane):
        return jnp.concatenate([tile] * lane_tiles(lane), axis=1)

    def received(codes, count, lane):
        exponent = codes[count * lane_tiles(lane)].astype(jnp.float32)
        return codes, jnp.exp2(exponent) * (1.0 / TOP)

    def decoded(part, lane, at):
        codes, unit = part
        count = lane_tiles(lane)
        value = jnp.concatenate([codes[at * count + tile] for tile in range(count)], axis=1)
        return value.astype(jnp.float32) * spread(unit, lane)

    def put(codes, lane, at, scaled):
        value = jnp.round(scaled).astype(jnp.int32).astype(jnp.int16)
        for tile in range(lane_tiles(lane)):
            codes[at * lane_tiles(lane) + tile] = value[:, tile * 128 : (tile + 1) * 128]

    def encode(lane, where, count, parts, codes):
        begin, width = lanes[lane]
        columns = pl.ds(begin, width)

        def largest(at, top):
            index = where(at) + (slice(None), columns)
            value = grads[index]
            for part in parts:
                value += decoded(part, lane, at)
            if parts:
                grads[index] = value
            return jnp.maximum(top, jnp.abs(value))
        exponent = exponent_of(lax.fori_loop(0, count, largest, jnp.zeros((owned, width), jnp.float32)))
        codes[count * lane_tiles(lane)] = exponent.astype(jnp.int32).astype(jnp.int16)
        factor = jnp.exp2(-exponent) * TOP

        def code(at):
            put(codes, lane, at, grads[where(at) + (slice(None), columns)] * spread(factor, lane))
        tiles(count, code)

    def code_copy(lane, slot, count, buffers, sems, axis, offset):
        part = slot + (pl.ds(0, count * lane_tiles(lane) + 1),)
        return remote(buffers[0].at[part], buffers[1].at[part], sems[0].at[slot], sems[1].at[slot], axis, offset)

    def large(lane, k, message):
        way = way_of(k)
        return code_copy(lane, (lane, k, message), RING, (sent1, got1), (r1_send, r1_recv), SCATTER[lane][0],
                         RING - way if message == 1 else way)

    def medium(lane, k):
        return code_copy(lane, (lane, k - 1), RING, (sent2, got2), (r2_send, r2_recv), SCATTER[lane][1], k)

    def small(lane, k):
        return code_copy(lane, (lane, k - 1), 1, (sent3, got3), (r3_send, r3_recv), SCATTER[lane][2], k)

    def scatter_large(lane, k, message):
        order = SCATTER[lane]
        way = way_of(k)
        row = on_ring(order[0], (2, RING - way, way)[message])
        middle = on_ring(order[1], k)
        parts = []
        if message == 2:
            large(lane, k, 0).wait_recv()
            parts = [received(got1.at[lane, k, 0], RING, lane)]
        encode(lane, lambda at: place(order, row, middle, at), RING, parts, sent1.at[lane, k, message])
        large(lane, k, message).start()

    def near_parts(lane, k):
        for message in (1, 2):
            large(lane, k, message).wait_recv()
        return [received(got1.at[lane, k, message], RING, lane) for message in (1, 2)]

    def scatter_middle(lane, k):
        order = SCATTER[lane]
        middle = on_ring(order[1], k)
        encode(lane, lambda at: place(order, me[order[0]], middle, at), RING, near_parts(lane, k),
               sent2.at[lane, k - 1])
        medium(lane, k).start()

    def own_parts(lane):
        for k in range(1, RING):
            medium(lane, k).wait_recv()
        return near_parts(lane, 0) + [received(got2.at[lane, slot], RING, lane) for slot in range(RING - 1)]

    def own_value(lane, parts, at):
        order = SCATTER[lane]
        value = grads[place(order, me[order[0]], me[order[1]], at) + (slice(None), pl.ds(*lanes[lane]))]
        for part in parts:
            value += decoded(part, lane, at)
        return value

    def scatter_small(lane, k, parts):
        value = own_value(lane, parts, on_ring(SCATTER[lane][2], k))
        exponent = exponent_of(jnp.abs(value))
        sent3[lane, k - 1, lane_tiles(lane)] = exponent.astype(jnp.int32).astype(jnp.int16)
        put(sent3.at[lane, k - 1], lane, 0, value * spread(jnp.exp2(-exponent) * TOP, lane))
        small(lane, k).start()

    def hidden_part(lane, offset):
        axis = GATHER[lane][2]
        columns = pl.ds(*gather_lanes[lane])
        index = tuple(on_ring(axis, offset) if dim == axis else slice(None) for dim in range(3))
        rows = weights[index + (slice(None), columns)].reshape(RING * RING * owned, gather_lanes[lane][1])
        value = lax.dot_general(
            rows, cot[:, columns], (((1,), (1,)), ((), ())), preferred_element_type=jnp.float32
        )
        dh_t[index] = dh_t[index] + value.reshape(RING, RING, owned, tokens)

    limit_mask = lax.broadcasted_iota(jnp.int32, (tokens, 1), 0) < limit
    quarter = RING * RING * owned

    def turn_back(at):
        value = scale * dh_t[at].reshape(quarter, tokens).T
        value = jnp.where(limit_mask, value, 0.0)
        dh[:, pl.ds(pl.multiple_of(at * quarter, quarter), quarter)] = value.astype(dh.dtype)

    every = range(LANES)

    def gather_next(k):
        for slot in range(2):
            for lane in every:
                gather_large(lane, k, slot).start()

    def gather_onward(k):
        for lane in every:
            gather_large(lane, k, 0).wait_recv()
            gather_large(lane, k, 2).start()

    load_w.wait()
    for offset in (1, 3, 2):
        for lane in every:
            gather_small(lane, 0, offset, ga_send, ga_recv).start()
    load_hid.wait()
    tiles(tokens // TILE, turn)

    def clear(at):
        dh_t[at] = jnp.zeros(dh_t.shape[1:], jnp.float32)
    tiles(RING, clear)
    for offset in (1, 3, 2):
        for lane in every:
            gather_small(lane, 0, offset, ga_send, ga_recv).wait_recv()
    for offset in (1, 3):
        for lane in every:
            gather_small(lane, 1, offset, gb_send, gb_recv).start()
    gather_next(0)
    load_cot.wait()

    def product_step(at):
        product(at)

        @pl.when(at == 5)
        def _():
            gather_halves()
            gather_next(1)
    tiles(cot.shape[1] // TILE, product_step)

    def near_and_far(step):
        k = part_of(step)
        for lane in every:
            scatter_large(lane, k, 0)
            scatter_large(lane, k, 1)
    tiles(RING, near_and_far)
    for lane in every:
        gather_half(lane, 0).wait_recv()
        gather_half(lane, 1).wait_recv()

    def with_far(step):
        k = part_of(step)
        for lane in every:
            scatter_large(lane, k, 2)
    tiles(RING, with_far)
    gather_onward(0)

    def second_stage(step):
        k = part_of(step)
        for lane in every:
            scatter_middle(lane, k)
    tiles(RING - 1, second_stage)
    gather_next(3)
    gather_next(2)
    for lane in every:
        hidden_part(lane, 0)
    for lane in every:
        parts = own_parts(lane)
        tiles(RING - 1, lambda step, lane=lane, parts=parts: scatter_small(lane, part_of(step), parts))
    gather_onward(1)
    gather_onward(3)
    gather_onward(2)

    for load in (load_mom, load_sec, load_srv):
        load.wait()
    shared = []
    for lane in range(LANES):
        begin, width = lanes[lane]
        columns = pl.ds(begin, width)
        parts = [received(got1.at[lane, 0, message], RING, lane) for message in (1, 2)]
        parts += [received(got2.at[lane, slot], RING, lane) for slot in range(RING - 1)]
        total = own_value(lane, parts, me[SCATTER[lane][2]])
        for slot in range(RING - 1):
            small(lane, slot + 1).wait_recv()
            total += decoded(received(got3.at[lane, slot], 1, lane), lane, 0)
        grad = scale * total
        first_new = beta_one * mom[:, columns] + (1.0 - beta_one) * grad
        squares_new = beta_two * sec[:, columns] + (1.0 - beta_two) * grad * grad
        step = first_new / bias_one / (jnp.sqrt(squares_new / bias_two) + epsilon)
        current = weights[me[0], me[1], me[2], :, columns].astype(jnp.float32)
        updated = current - learn_rate * (step + decay_rate * current)
        delta[core, :, columns] = (updated - current).astype(delta.dtype)
        part = delta.at[core, :, columns]
        shared.append(pltpu.make_async_remote_copy(
            src_ref=part, dst_ref=part, send_sem=d_send.at[lane], recv_sem=d_recv.at[lane],
            device_id={"expert": 1 - core}, device_id_type=MESH,
        ))
        shared[lane].start()
        nw[:, columns] = updated.astype(nw.dtype)
        nm[:, columns] = first_new
        ns[:, columns] = squares_new

    def near_slab(step):
        for lane in every:
            hidden_part(lane, 1 + 2 * step)
    for k in range(RING):
        for lane in every:
            gather_large(lane, k, 1).wait_recv()
    tiles(2, near_slab)
    for lane in range(LANES):
        begin, width = lanes[lane]
        columns = pl.ds(begin, width)
        shared[lane].wait_recv()
        choices = [delta[expert, :, columns].astype(jnp.float32) for expert in range(2)]
        for replica in range(srv.shape[0]):
            pick = jnp.full((owned, width), placement[core, replica], jnp.int32) == 0
            incoming = jnp.where(pick, choices[0], choices[1])
            so[replica, :, columns] = (srv[replica, :, columns].astype(jnp.float32) + incoming).astype(so.dtype)

    def sent_all(k):
        for lane in every:
            for slot in range(2):
                gather_large(lane, k, slot).wait_send()
            for slot in range(3):
                large(lane, k, slot).wait_send()

            @pl.when(k > 0)
            def _():
                gather_small(lane, 0, k, ga_send, ga_recv).wait_send()
                medium(lane, k).wait_send()
                small(lane, k).wait_send()
    tiles(RING, sent_all)
    for lane in every:
        for half, offset in enumerate((1, 3)):
            gather_small(lane, 1, offset, gb_send, gb_recv).wait_send()
            gather_half(lane, half).wait_send()
    for copy in shared:
        copy.wait_send()

    def gathered(k):
        for lane in every:
            gather_large(lane, k, 2).wait()
    tiles(RING, gathered)
    for lane in every:
        hidden_part(lane, 2)
    tiles(RING, turn_back)


def store(*refs):
    count = len(refs) // 2
    sem = refs[2 * count]
    copies = [pltpu.make_async_copy(refs[at], refs[count + at], sem.at[at]) for at in range(count)]
    for copy in copies:
        copy.start()
    for copy in copies:
        copy.wait()


def stored(arrays):
    anywhere = pl.BlockSpec(memory_space=pl.ANY)
    return pl.pallas_call(
        store,
        out_shape=tuple(jax.ShapeDtypeStruct(array.shape, array.dtype) for array in arrays),
        in_specs=[anywhere] * len(arrays),
        out_specs=[anywhere] * len(arrays),
        scratch_shapes=[pltpu.SemaphoreType.DMA((len(arrays),))],
        compiler_params=pltpu.CompilerParams(vmem_limit_bytes=2**20),
    )(*arrays)


def on_device(hidden, cotangent, counts, placement, weight, moment, second, serving):
    tokens, rows = hidden.shape[1:]
    width = cotangent.shape[2]
    owned = weight.shape[1]
    copies = serving.shape[1]
    gather_lanes = lane_columns(width, 0)
    lanes = lane_columns(width, 1)
    most = max(count for _, count in lanes) // 128
    scale = width ** (-0.5)
    anywhere = pl.BlockSpec(memory_space=pl.ANY)
    scalars = pl.BlockSpec(memory_space=pltpu.SMEM)
    f32, bf16, i16 = jnp.float32, jnp.bfloat16, jnp.int16
    dma = pltpu.SemaphoreType.DMA
    outs = pl.pallas_call(
        functools.partial(fused, scale, gather_lanes, lanes),
        out_shape=(
            pltpu.VMEM((tokens, rows), bf16),
            pltpu.VMEM((owned, width), bf16),
            pltpu.VMEM((owned, width), f32),
            pltpu.VMEM((owned, width), f32),
            pltpu.VMEM((copies, owned, width), bf16),
        ),
        in_specs=[scalars, scalars] + [anywhere] * 6,
        out_specs=[pl.BlockSpec(memory_space=pltpu.VMEM)] * 5,
        scratch_shapes=[
            pltpu.VMEM((RING, RING, RING, owned, width), bf16),
            pltpu.VMEM((tokens, rows), bf16),
            pltpu.VMEM((rows, tokens), bf16),
            pltpu.VMEM((tokens, width), bf16),
            pltpu.VMEM((RING, RING, RING, owned, width), f32),
            pltpu.VMEM((RING, RING, RING, owned, tokens), f32),
            pltpu.VMEM((owned, width), f32),
            pltpu.VMEM((owned, width), f32),
            pltpu.VMEM((copies, owned, width), bf16),
            pltpu.VMEM((2, owned, width), bf16),
            pltpu.VMEM((LANES, RING, 3, RING * most + 1, owned, 128), i16),
            pltpu.VMEM((LANES, RING, 3, RING * most + 1, owned, 128), i16),
            pltpu.VMEM((LANES, 3, RING * most + 1, owned, 128), i16),
            pltpu.VMEM((LANES, 3, RING * most + 1, owned, 128), i16),
            pltpu.VMEM((LANES, 3, most + 1, owned, 128), i16),
            pltpu.VMEM((LANES, 3, most + 1, owned, 128), i16),
        ]
        + [dma((LANES, 3))] * 2
        + [dma((LANES, RING))] * 2
        + [dma((LANES, RING, 3))] * 4
        + [dma((LANES, 3))] * 4
        + [dma((LANES,))] * 2
        + [dma((6,))],
        compiler_params=pltpu.CompilerParams(
            collective_id=0, has_side_effects=True, vmem_limit_bytes=56 * 2**20
        ),
        cost_estimate=pl.CostEstimate(flops=4 * tokens * rows * width, bytes_accessed=2**25, transcendentals=0),
    )(counts, placement, hidden[0], cotangent[0], weight[0], moment[0], second[0], serving[0])
    return tuple(out[None] for out in stored(outs))


def solution(mesh):
    torus = Mesh(
        mesh.devices.reshape(RING, RING, RING, mesh.shape["expert"]), ("dp_0", "dp_1", "dp_2", "expert")
    )
    return jax.shard_map(
        on_device,
        mesh=torus,
        in_specs=(
            P("expert", DP, None),
            P("expert", DP, None),
            P("expert", DP),
            P(),
            P("expert", DP, None),
            P("expert", DP, None),
            P("expert", DP, None),
            P("expert", None, DP, None),
        ),
        out_specs=(
            P("expert", DP, None),
            P("expert", DP, None),
            P("expert", DP, None),
            P("expert", DP, None),
            P("expert", None, DP, None),
        ),
        check_vma=False,
    )
```
